512 devices in a mesh: rows: 16 (over x_lo, z), cols: 32 (over y, x_hi, core).
Axes of the slice: x: 4 (x_hi: 2, x_lo: 2; x = x_hi * 2 + x_lo), y: 8, z: 8, core: 2. Of those that a mesh axis runs over, the one named last changes fastest.
Arguments:
- tokens: bfloat16 [128, 1024, 192], P('rows', 'cols'), may hold values from -60 to 60
- region_ids: int32 [128, 1024], P('rows', 'cols'), may hold values from 0 to 2
- upper_rim: bfloat16 [4, 1024, 192], P(None, 'cols'), may hold values from -60 to 60
- upper_ids: int32 [4, 1024], P(None, 'cols'), may hold values from 0 to 2
- lower_rim: bfloat16 [4, 1024, 192], P(None, 'cols'), may hold values from -60 to 60
- lower_ids: int32 [4, 1024], P(None, 'cols'), may hold values from 0 to 2
- cotangent: bfloat16 [128, 1024, 192], P('rows', 'cols'), may hold values from -6 to 6
- qkv_weight: bfloat16 [2, 192, 576], replicated, may hold values from -0.4375 to 0.4375
- proj_weight: bfloat16 [2, 192, 192], replicated, may hold values from -0.4375 to 0.4375
- inner_weight: bfloat16 [2, 192, 768], replicated, may hold values from -0.4375 to 0.4375
- outer_weight: bfloat16 [2, 768, 192], replicated, may hold values from -0.21875 to 0.21875
- bias_table: float32 [2, 225, 6], replicated, may hold values from -4 to 400
Outputs:
- token_grad: bfloat16 [128, 1024, 192], P('rows', 'cols')
- qkv_grad: float32 [2, 192, 576], P(None, 'rows', 'cols')
- proj_grad: float32 [2, 192, 192], P(None, 'rows', 'cols')
- inner_grad: float32 [2, 192, 768], P(None, 'rows', 'cols')
- outer_grad: float32 [2, 768, 192], P(None, 'rows', 'cols')
- table_grad: float32 [2, 225, 6], replicated
The draws below stay inside these ranges and needn't reach their ends.
All inputs are finite; a program needn't handle non-finite values.
Results may differ from the reference program's by a relative error of at most 0.03.
Values may be sent and summed in bfloat16 or wider, within the bound.
A program may use at most 64 MiB of HBM per device.

```python
import math
import jax
import jax.numpy as jnp
from jax import lax

C = 192
HEADS = 6
HID = 768
WIN = 8
HALF = 4
BIAS_LEN = 225
NROWS = 128
NCOL = 1024
NTILES = 512


def feature_field(key, tag_number, shape):
    chan_key = jax.random.fold_in(key, 101)
    own_key = jax.random.fold_in(key, tag_number)
    scale_key, raw_key = jax.random.split(own_key)
    channel_scale = 0.5 * jnp.exp(jax.random.uniform(chan_key, (C,), jnp.float32) * math.log(10.0))
    token_scale = 0.3 * jnp.exp(jax.random.uniform(scale_key, shape[:-1] + (1,), jnp.float32) * math.log(10.0))
    raw_values = jnp.clip(jax.random.normal(raw_key, shape, jnp.float32), -4.0, 4.0)
    return raw_values * token_scale * channel_scale


def draw_tokens(key, part):
    return feature_field(key, 1, (NROWS, NCOL, C)).astype(jnp.bfloat16)


def draw_upper_rim(key, part):
    return feature_field(key, 2, (HALF, NCOL, C)).astype(jnp.bfloat16)


def draw_lower_rim(key, part):
    return feature_field(key, 3, (HALF, NCOL, C)).astype(jnp.bfloat16)


def draw_bias_table(key, part):
    table_key = jax.random.fold_in(key, 7)
    raw_values = jnp.clip(jax.random.normal(table_key, (2, BIAS_LEN, HEADS), jnp.float32), -4.0, 4.0)
    return raw_values


def place_ends(drawn, key, smallest, high):
    spot = [jax.random.randint(jax.random.fold_in(key, axis), (), 0, length) for axis, length in enumerate(drawn.shape)]
    widest = drawn.shape.index(max(drawn.shape))
    next_to = spot[:widest] + [(spot[widest] + 1) % drawn.shape[widest]] + spot[widest + 1:]
    return drawn.at[tuple(spot)].set(smallest).at[tuple(next_to)].set(high)


def raised(result, stream_key, source, target, blocks, factor):
    def block_of(position):
        return (jnp.arange(result.shape[position]) // (result.shape[position] // blocks)).reshape((-1,) + (1,) * (result.ndim - 1 - position))

    near = jax.random.permutation(stream_key, blocks)[block_of(target)]
    second = (block_of(target) + blocks // 2) % blocks
    return jnp.where((block_of(source) == near) | (block_of(source) == second), factor * result, result)


def shard_levels(stream_key, shape, shards, least, high):
    def one(axis_at, shards_of):
        draws = jax.random.uniform(jax.random.fold_in(jax.random.fold_in(stream_key, 6), axis_at), (shards_of,), jnp.float32, least / len(shards), high / len(shards))
        return jnp.repeat(jnp.exp(draws), shape[axis_at] // shards_of).reshape((-1,) + (1,) * (len(shape) - axis_at - 1))

    level = one(*shards[0])
    for cut in shards[1:]:
        level = level * one(*cut)
    return level


def normal_values(key, dims, width, reach, shards=(), kind=jnp.bfloat16):
    level = shard_levels(key, dims, shards, -0.22, 0.18) if shards else 1.0
    entries = jax.random.normal(key, dims, jnp.float32) * width * level
    return jnp.minimum(jnp.maximum(entries, -reach), reach).astype(kind)


def gaussian_with(key, extent, scale, bound, pieces, heavy, kind=jnp.bfloat16):
    array = scale * jax.random.normal(key, extent, jnp.float32)
    if pieces:
        array = array * shard_levels(key, extent, pieces, -0.22, 0.18)
    return jnp.clip(raised(array, jax.random.fold_in(key, 3), *heavy), -bound, bound).astype(kind)


def setup_inputs(seed: int = 0) -> dict:
    splits = jax.random.split(jax.random.key(seed), 13)
    return {
        "tokens": draw_tokens(jax.random.fold_in(splits[12], 71), 0),
        "region_ids": place_ends(jax.random.randint(splits[1], (NROWS, NCOL), 0, 3), jax.random.fold_in(splits[1], 1), 0, 2).astype(jnp.int32),
        "upper_rim": draw_upper_rim(jax.random.fold_in(splits[12], 71), 0),
        "upper_ids": place_ends(jax.random.randint(splits[3], (HALF, NCOL), 0, 3), jax.random.fold_in(splits[3], 1), 0, 2).astype(jnp.int32),
        "lower_rim": draw_lower_rim(jax.random.fold_in(splits[12], 71), 0),
        "lower_ids": place_ends(jax.random.randint(splits[5], (HALF, NCOL), 0, 3), jax.random.fold_in(splits[5], 1), 0, 2).astype(jnp.int32),
        "cotangent": gaussian_with(splits[6], (NROWS, NCOL, C), 1.0, 6.0, ((0, 16), (1, 32)), (1, 2, 32, 2.75)),
        "qkv_weight": normal_values(splits[7], (2, C, 3 * C), C ** -0.5, 0.4375),
        "proj_weight": normal_values(splits[8], (2, C, C), C ** -0.5, 0.4375),
        "inner_weight": normal_values(splits[9], (2, C, HID), C ** -0.5, 0.4375),
        "outer_weight": normal_values(splits[10], (2, HID, C), HID ** -0.5, 0.21875),
        "bias_table": draw_bias_table(jax.random.fold_in(splits[12], 71), 0),
    }


EPS = 1e-05
MASKED = -1000000000.0

def rounded(values):
    return lax.optimization_barrier(values.astype(jnp.bfloat16)).astype(jnp.float32)

def normalize(values):
    center = lax.optimization_barrier(jnp.mean(values, axis=-1, keepdims=True))
    shifted = values - center
    spread = lax.optimization_barrier(jnp.mean(shifted * shifted, axis=-1, keepdims=True))
    return shifted * lax.rsqrt(spread + EPS)

def norm_back(source, grad_norm):
    _, pullback = jax.vjp(normalize, source.astype(jnp.float32))
    return pullback(grad_norm)[0]

def by_transpose(left, right):
    return lax.dot_general(left, right, (((1,), (1,)), ((), ())), preferred_element_type=jnp.float32)

def over_rows(left, right):
    return lax.dot_general(left, right, (((0,), (0,)), ((), ())), preferred_element_type=jnp.float32)

def windows(surface):
    grid_rows, grid_cols = (surface.shape[0], surface.shape[1])
    trailing = surface.shape[2:]
    blocked = surface.reshape((grid_rows // WIN, WIN, grid_cols // WIN, WIN) + trailing)
    permute = (0, 2, 1, 3) + tuple(range(4, 4 + len(trailing)))
    return blocked.transpose(permute).reshape((grid_rows // WIN * (grid_cols // WIN), WIN * WIN) + trailing)

def unwindows(framed, grid_rows, grid_cols):
    trailing = framed.shape[2:]
    blocked = framed.reshape((grid_rows // WIN, grid_cols // WIN, WIN, WIN) + trailing)
    permute = (0, 2, 1, 3) + tuple(range(4, 4 + len(trailing)))
    return blocked.transpose(permute).reshape((grid_rows, grid_cols) + trailing)

def relative_onehot():
    places = jnp.arange(WIN * WIN, dtype=jnp.int32)
    pos_row = places // WIN
    pos_col = places % WIN
    lookup = (pos_row[:, None] - pos_row[None, :] + WIN - 1) * (2 * WIN - 1) + pos_col[:, None] - pos_col[None, :] + WIN - 1
    return (lookup[:, :, None] == jnp.arange(BIAS_LEN, dtype=jnp.int32)[None, None, :]).astype(jnp.float32)

def attend(normed_win, ids_win, qkv_weight, pos_bias):
    window_count, window_size, channels = normed_win.shape
    head_count = pos_bias.shape[0]
    head_size = channels // head_count
    score_scale = head_size ** (-0.5)
    qkv_all = jnp.dot(normed_win.reshape(window_count * window_size, channels), qkv_weight, preferred_element_type=jnp.float32)
    qkv_all = rounded(qkv_all).reshape(window_count, window_size, 3, head_count, head_size)
    scores = jnp.einsum('nqhd,nkhd->nhqk', qkv_all[:, :, 0], qkv_all[:, :, 1])
    scores = scores * score_scale + pos_bias[None]
    same_region = ids_win[:, :, None] == ids_win[:, None, :]
    scores = jnp.where(same_region[:, None], scores, MASKED)
    row_max = lax.optimization_barrier(jnp.max(scores, axis=-1, keepdims=True))
    exponent = jnp.exp(scores - row_max)
    attn_probs = exponent / lax.optimization_barrier(jnp.sum(exponent, axis=-1, keepdims=True))
    attn_out = jnp.einsum('nhqk,nkhd->nqhd', rounded(attn_probs), qkv_all[:, :, 2])
    return (qkv_all, attn_probs, attn_out.astype(jnp.bfloat16).reshape(window_count, window_size, channels))

def attend_back(normed_win, qkv_all, attn_probs, grad_out, qkv_weight):
    window_count, window_size, channels = normed_win.shape
    head_count, head_size = (qkv_all.shape[3], qkv_all.shape[4])
    score_scale = head_size ** (-0.5)
    grad_heads = grad_out.astype(jnp.float32).reshape(window_count, window_size, head_count, head_size)
    grad_probs = jnp.einsum('nqhd,nkhd->nhqk', grad_heads, qkv_all[:, :, 2])
    grad_scores = attn_probs * (grad_probs - lax.optimization_barrier(jnp.sum(grad_probs * attn_probs, axis=-1, keepdims=True)))
    grad_bias = lax.optimization_barrier(jnp.sum(grad_scores, axis=0))
    scores_low = rounded(grad_scores)
    grad_query = jnp.einsum('nhqk,nkhd->nqhd', scores_low, qkv_all[:, :, 1]) * score_scale
    grad_key = jnp.einsum('nhqk,nqhd->nkhd', scores_low, qkv_all[:, :, 0]) * score_scale
    grad_value = jnp.einsum('nhqk,nqhd->nkhd', rounded(attn_probs), grad_heads)
    grad_qkv = jnp.stack([grad_query, grad_key, grad_value], axis=2).astype(jnp.bfloat16)
    grad_qkv = grad_qkv.reshape(window_count * window_size, 3 * channels)
    flattened = normed_win.reshape(window_count * window_size, channels)
    grad_norm = by_transpose(grad_qkv, qkv_weight)
    grad_weight = over_rows(flattened, grad_qkv)
    return (grad_norm.reshape(window_count, window_size, channels), grad_weight, grad_bias)

def mixer_forward(surface, region, qkv_weight, table):
    grid_rows, grid_cols = (surface.shape[0], surface.shape[1])
    normed = normalize(surface.astype(jnp.float32)).astype(jnp.bfloat16)
    pos_bias = jnp.einsum('ijb,bh->hij', relative_onehot(), table, precision=lax.Precision.HIGHEST)
    qkv_all, attn_probs, attn_out = attend(windows(normed), windows(region), qkv_weight, pos_bias)
    return (normed, qkv_all, attn_probs, unwindows(attn_out, grid_rows, grid_cols))

def mixer_backward(surface, normed, qkv_all, attn_probs, grad_mix, qkv_weight):
    grid_rows, grid_cols = (surface.shape[0], surface.shape[1])
    grad_norm, grad_weight, grad_bias = attend_back(windows(normed), qkv_all, attn_probs, windows(grad_mix), qkv_weight)
    grad_surface = norm_back(surface, unwindows(grad_norm, grid_rows, grid_cols))
    grad_table = jnp.einsum('ijb,hij->bh', relative_onehot(), grad_bias, precision=lax.Precision.HIGHEST)
    return (grad_surface, grad_weight, grad_table)

def channel_forward(middle, inner_w, outer_w):
    normed = normalize(middle.astype(jnp.float32)).astype(jnp.bfloat16)
    hidden_pre = jnp.dot(normed, inner_w, preferred_element_type=jnp.float32)
    hidden_act = jax.nn.gelu(hidden_pre, approximate=False).astype(jnp.bfloat16)
    output = (middle.astype(jnp.float32) + jnp.dot(hidden_act, outer_w, preferred_element_type=jnp.float32)).astype(jnp.bfloat16)
    return (normed, hidden_pre, hidden_act, output)

def channel_backward(middle, normed, hidden_pre, hidden_act, grad_out, inner_w, outer_w):
    grad_act = by_transpose(grad_out, outer_w)
    grad_outer = over_rows(hidden_act, grad_out)
    _, pullback = jax.vjp(lambda inputs: jax.nn.gelu(inputs, approximate=False), hidden_pre)
    grad_pre = pullback(grad_act)[0].astype(jnp.bfloat16)
    grad_norm = by_transpose(grad_pre, inner_w)
    grad_inner = over_rows(normed, grad_pre)
    grad_middle = (grad_out.astype(jnp.float32) + norm_back(middle, grad_norm)).astype(jnp.bfloat16)
    return (grad_middle, grad_inner, grad_outer)

def reference(tokens, region_ids, upper_rim, upper_ids, lower_rim, lower_ids, cotangent, qkv_weight, proj_weight, inner_weight, outer_weight, bias_table):
    grid_rows, grid_cols, channels = tokens.shape
    normed_one, qkv_one, probs_one, mix_one = mixer_forward(tokens, region_ids, qkv_weight[0], bias_table[0])
    mix_flat_one = mix_one.reshape(grid_rows * grid_cols, channels)
    middle_one = (tokens.reshape(-1, channels).astype(jnp.float32) + jnp.dot(mix_flat_one, proj_weight[0], preferred_element_type=jnp.float32)).astype(jnp.bfloat16)
    chan_one = channel_forward(middle_one, inner_weight[0], outer_weight[0])
    first_out = chan_one[3].reshape(grid_rows, grid_cols, channels)
    extended = jnp.concatenate([upper_rim, first_out, lower_rim], axis=0)
    ext_region = jnp.concatenate([upper_ids, region_ids, lower_ids], axis=0)
    shifted = jnp.roll(extended, -HALF, axis=1)
    shifted_ids = jnp.roll(ext_region, -HALF, axis=1)
    normed_two, qkv_two, probs_two, mix_ext = mixer_forward(shifted, shifted_ids, qkv_weight[1], bias_table[1])
    mix_two = jnp.roll(mix_ext, HALF, axis=1)[HALF:HALF + grid_rows]
    mix_flat_two = mix_two.reshape(grid_rows * grid_cols, channels)
    middle_two = (chan_one[3].astype(jnp.float32) + jnp.dot(mix_flat_two, proj_weight[1], preferred_element_type=jnp.float32)).astype(jnp.bfloat16)
    chan_two = channel_forward(middle_two, inner_weight[1], outer_weight[1])
    grad_out = cotangent.reshape(-1, channels)
    grad_mid_two, inner_two, outer_two = channel_backward(middle_two, chan_two[0], chan_two[1], chan_two[2], grad_out, inner_weight[1], outer_weight[1])
    proj_two = over_rows(mix_flat_two, grad_mid_two)
    grad_mix_two = by_transpose(grad_mid_two, proj_weight[1]).astype(jnp.bfloat16).reshape(grid_rows, grid_cols, channels)
    grad_mix_ext = jnp.roll(jnp.pad(grad_mix_two, ((HALF, HALF), (0, 0), (0, 0))), -HALF, axis=1)
    grad_shift, qkv_two_grad, table_two = mixer_backward(shifted, normed_two, qkv_two, probs_two, grad_mix_ext, qkv_weight[1])
    folded = jnp.roll(grad_shift, HALF, axis=1)[HALF:HALF + grid_rows]
    grad_first = (grad_mid_two.reshape(grid_rows, grid_cols, channels).astype(jnp.float32) + folded).astype(jnp.bfloat16)
    grad_mid_one, inner_one, outer_one = channel_backward(middle_one, chan_one[0], chan_one[1], chan_one[2], grad_first.reshape(-1, channels), inner_weight[0], outer_weight[0])
    proj_one = over_rows(mix_flat_one, grad_mid_one)
    grad_mix_one = by_transpose(grad_mid_one, proj_weight[0]).astype(jnp.bfloat16).reshape(grid_rows, grid_cols, channels)
    grad_tokens, qkv_one_grad, table_one = mixer_backward(tokens, normed_one, qkv_one, probs_one, grad_mix_one, qkv_weight[0])
    token_grad = (grad_mid_one.reshape(grid_rows, grid_cols, channels).astype(jnp.float32) + grad_tokens).astype(jnp.bfloat16)
    tile_count = NTILES * 1.0
    qkv_grad = jnp.stack([qkv_one_grad, qkv_two_grad]) / tile_count
    proj_grad = jnp.stack([proj_one, proj_two]) / tile_count
    inner_grad = jnp.stack([inner_one, inner_two]) / tile_count
    outer_grad = jnp.stack([outer_one, outer_two]) / tile_count
    table_grad = jnp.stack([table_one, table_two]) / tile_count
    return (token_grad, qkv_grad, proj_grad, inner_grad, outer_grad, table_grad)
```

```python
import functools
import math
import types

import jax
import jax.numpy as jnp
from jax import lax
from jax.experimental import pallas as pl
from jax.experimental.pallas import tpu as pltpu
from jax.sharding import PartitionSpec as P

C = 192
HEADS = 6
HD = 32
HID = 768
WIN = 8
HALF = 4
EPS = 1e-05
MASKED = -1000000000.0
SCALE = HD**-0.5
CW = 256
CHUNK = 80
F32 = jnp.float32
BF16 = jnp.bfloat16
MESH = pl.DeviceIdType.MESH


def dot(a, b):
    return lax.dot_general(a, b, (((1,), (0,)), ((), ())), preferred_element_type=F32)


def dot_t(a, b):
    return lax.dot_general(a, b, (((1,), (1,)), ((), ())), preferred_element_type=F32)


def t_dot(a, b):
    return lax.dot_general(a, b, (((0,), (0,)), ((), ())), preferred_element_type=F32)


def iota(shape, dim):
    return lax.broadcasted_iota(jnp.int32, shape, dim)


def stats(values):
    center = jnp.sum(values, axis=-1, keepdims=True) * (1.0 / C)
    shifted = values - center
    spread = jnp.sum(shifted * shifted, axis=-1, keepdims=True) * (1.0 / C)
    inverse = lax.rsqrt(spread + EPS)
    return shifted * inverse, inverse


def norm_back(values, grad):
    hat, inverse = stats(values)
    mean_grad = jnp.sum(grad, axis=-1, keepdims=True) * (1.0 / C)
    mean_dot = jnp.sum(grad * hat, axis=-1, keepdims=True) * (1.0 / C)
    return inverse * (grad - mean_grad - hat * mean_dot)


def by_heads(values):
    lane_head = iota(values.shape, 1) // HD
    zero = jnp.zeros_like(values)
    return jnp.concatenate([jnp.where(lane_head == h, values, zero) for h in range(HEADS)], axis=0)


def gather_heads(stacked):
    lane_head = iota((64, C), 1) // HD
    total = jnp.zeros((64, C), F32)
    for h in range(HEADS):
        total = jnp.where(lane_head == h, stacked[h * 64 : h * 64 + 64], total)
    return total


def head_reduce(scores, reduce, fill):
    pieces = []
    for pair in range(3):
        part = scores[:, pair * 128 : pair * 128 + 128]
        first = iota(part.shape, 1) < 64
        low = reduce(jnp.where(first, part, fill), axis=-1, keepdims=True)
        high = reduce(jnp.where(first, fill, part), axis=-1, keepdims=True)
        pieces.append(jnp.where(first, low, high))
    return jnp.concatenate(pieces, axis=1)


def softmax_window(q, k_heads, z_q, z_heads, bias):
    scores = dot_t(q, k_heads) * SCALE + bias
    scores = jnp.where(dot_t(z_q, z_heads) > 0.5, scores, MASKED)
    exponent = jnp.exp(scores - head_reduce(scores, jnp.max, -jnp.inf))
    return exponent / head_reduce(exponent, jnp.sum, 0.0)


def tile_ids(ids):
    z = (iota(ids.shape, 1).astype(F32) == ids).astype(BF16)
    return z, jnp.concatenate([z] * HEADS, axis=0)


def gelu_parts(pre):
    cdf = 0.5 * (1.0 + lax.erf(pre * (1.0 / math.sqrt(2.0))))
    slope = cdf + pre * (jnp.exp(-0.5 * pre * pre) * (1.0 / math.sqrt(2.0 * math.pi)))
    return pre * cdf, slope


def split(values):
    high = values.astype(BF16)
    rest = values - high.astype(F32)
    middle = rest.astype(BF16)
    low = (rest - middle.astype(F32)).astype(BF16)
    return jnp.concatenate([high, middle, low], axis=0)


def joined(pieces):
    n = pieces.shape[0] // 3
    return pieces[0:n] + pieces[n : 2 * n] + pieces[2 * n :]


def offset_onehots(out_ref):
    lane = iota((1, 128), 1)
    row = iota((256, 128), 0)
    for ci in range(WIN):
        offset = jnp.where(lane < 120, (14 - lane // 8) * 15 + (ci - lane % 8 + 7), -1)
        out_ref[ci] = (row == offset).astype(BF16)


def spread_bias(R):
    R.tab[...] = jnp.zeros((16, 256), F32)
    for b in range(2):
        R.tab[b * 8 : b * 8 + 6, 0:225] = R.table[:, b, :]
    pieces = split(R.tab[...])
    per_column = [joined(dot(pieces, R.offsets[ci])) for ci in range(WIN)]
    first = iota((8, 128), 1) < 64
    for b in range(2):
        per_head = [
            jnp.concatenate([per_column[ci][b * 8 + h : b * 8 + h + 1] for ci in range(WIN)], axis=0)
            for h in range(HEADS)
        ]
        for ri in range(WIN):
            shift = (7 - ri) * 8
            for pair in range(3):
                low = pltpu.roll(per_head[2 * pair], (128 - shift) % 128, 1)
                high = pltpu.roll(per_head[2 * pair + 1], (64 - shift) % 128, 1)
                R.bias[b, ri * 8 : ri * 8 + 8, pair * 128 : pair * 128 + 128] = jnp.where(first, low, high)


def fold_bias(grad_ref, offsets):
    first = iota((8, 128), 1) < 64
    per_head = [jnp.zeros((8, 128), F32) for _ in range(HEADS)]
    for ri in range(WIN):
        shift = (7 - ri) * 8
        for pair in range(3):
            part = grad_ref[ri * 8 : ri * 8 + 8, pair * 128 : pair * 128 + 128]
            low = pltpu.roll(jnp.where(first, part, 0.0), shift % 128, 1)
            high = pltpu.roll(jnp.where(first, 0.0, part), (shift + 64) % 128, 1)
            per_head[2 * pair] = per_head[2 * pair] + low
            per_head[2 * pair + 1] = per_head[2 * pair + 1] + high
    total = jnp.zeros((8, 256), F32)
    for ci in range(WIN):
        rows = jnp.concatenate([per_head[h][ci : ci + 1] for h in range(HEADS)] + [jnp.zeros((2, 128), F32)], axis=0)
        total = total + joined(dot_t(split(rows), offsets[ci]))
    return total


def place():
    r = lax.axis_index("rows")
    c = lax.axis_index("cols")
    return r, c


class Net:
    def __init__(self):
        r, c = place()
        self.r, self.c = r, c
        self.x_lo, self.z = r // 8, r % 8
        self.y, self.x_hi, self.core = c // 4, (c // 2) % 2, c % 2
        self.x = self.x_hi * 2 + self.x_lo

    def near(self, dr, dc):
        return ((self.r + dr + 16) % 16, (self.c + dc + 32) % 32)

    def partner(self):
        return (self.r, self.c + 1 - 2 * self.core)

    def at_x(self, x):
        return ((x % 2) * 8 + self.z, self.y * 4 + (x // 2) * 2 + self.core)

    def at_y(self, y):
        return (self.r, y * 4 + self.x_hi * 2 + self.core)

    def at_z(self, z):
        return (self.x_lo * 8 + z, self.c)

    def everyone(self):
        peers = [self.near(dr, dc) for dr, dc in SIDES] + [self.partner()]
        peers += [self.at_x((self.x + d) % 4) for d in range(1, 4)]
        peers += [self.at_y((self.y + d) % 8) for d in range(1, 8)]
        peers += [self.at_z((self.z + d) % 8) for d in range(1, 8)]
        return peers


SIDES = ((-1, 0), (1, 0), (0, -1), (0, 1), (-1, -1), (-1, 1), (1, -1), (1, 1))
SIDE_ROWS = (128, 128, 64, 64, 16, 16, 16, 16)
BACK_ROWS = (128, 128, 32, 32, 16, 16, 16, 16)


def remote(src, dst, send, recv, device):
    return pltpu.make_async_remote_copy(
        src_ref=src, dst_ref=dst, send_sem=send, recv_sem=recv, device_id=device, device_id_type=MESH
    )


def body(*refs):
    R = types.SimpleNamespace(**jax.tree.unflatten(STRUCTURE, refs[COUNT:]))
    R.tokens, R.ids, R.upper, R.upper_ids, R.lower, R.lower_ids, R.cot = refs[:7]
    R.qkv_w, R.proj_w, R.inner_w, R.outer_w, R.table, R.token_grad, R.qkv_grad = refs[7:14]
    R.proj_grad, R.inner_grad, R.outer_grad, R.table_grad = refs[14:COUNT]
    N = Net()

    barrier = pltpu.get_barrier_semaphore()
    peers = N.everyone()
    for peer in peers:
        pl.semaphore_signal(barrier, inc=1, device_id=peer, device_id_type=MESH)

    setup(R)
    forward_one(R)
    pl.semaphore_wait(barrier, len(peers))
    exchange_forward(R, N)
    forward_two(R)
    attend_back_two(R)
    send_back(R, N)
    grads_of(R, N, 1)
    start_core(R, N, 1)
    receive_back(R, N)
    channel_back_one(R)
    start_x(R, N, 1)
    attend_back_one(R)
    start_y(R, N, 1)
    finish_one(R)
    grads_of(R, N, 0)
    start_core(R, N, 0)
    start_z(R, N, 1)
    start_x(R, N, 0)
    finish_z(R, N, 1)
    start_y(R, N, 0)
    start_z(R, N, 0)
    finish_z(R, N, 0)
    finish_table(R)


def select_column(rows, order, ids):
    n = ids.shape[0]
    row_of, col_of = order
    pick = (iota((rows, n), 1) == row_of(iota((rows, n), 0))).astype(BF16)
    spread = dot(pick, ids.astype(F32).astype(BF16))
    keep = iota((rows, 32), 1) == col_of(iota((rows, 32), 0))
    column = jnp.sum(jnp.where(keep, spread, 0.0), axis=-1, keepdims=True)
    return jnp.broadcast_to(column, (rows, 128))


def setup(R):
    offset_onehots(R.offsets)
    spread_bias(R)
    for b in range(2):
        for i, ref in enumerate((R.wq, R.wk, R.wv)):
            ref[b] = R.qkv_w[b][:, i * C : i * C + C]
    for r in range(8):
        row = R.tokens[r].astype(F32)
        for w in range(4):
            R.x1[w * 64 + r * 8 : w * 64 + r * 8 + 8, :] = row[w * 8 : w * 8 + 8]
    by_window = (lambda t: (t // 8) % 8, lambda t: (t // 64) * 8 + t % 8)
    by_row = (lambda t: t // 32, lambda t: t % 32)
    R.id1[...] = select_column(256, by_window, R.ids[...])
    R.rim_id[0] = select_column(128, by_row, R.upper_ids[...])
    R.rim_id[1] = select_column(128, by_row, R.lower_ids[...])
    lane = iota((1, 1024), 1)
    inside = lane % 128
    row = (lane // 128 % 2 * 8 + inside // 12) * 48 + lane // 256 * 12 + inside % 12
    row = jnp.where(inside < 96, row, -1)
    R.pick_hid[...] = (iota((HID, 1024), 0) == row).astype(BF16)
    lane = iota((1, 256), 1)
    inside = lane % 128
    row = jnp.where(inside < 96, lane // 128 * 96 + inside, -1)
    R.pick_ch[...] = (iota((C, 256), 0) == row).astype(BF16)
    out = iota((4 * CHUNK, 1), 0)
    q, k = out // CHUNK, out % CHUNK
    hid = (k - 48) // 6
    col = jnp.where(
        k < 18,
        18 * q + k,
        jnp.where(
            k < 24,
            72 + 6 * q + k - 18,
            jnp.where(k < 48, 96 + 24 * q + k - 24, 192 + 24 * hid + 6 * q + (k - 48 - 6 * hid)),
        ),
    )
    col = jnp.where(k < 72, col, -1)
    R.cut[...] = (iota((4 * CHUNK, 288), 1) == col).astype(BF16)


def forward_one(R):
    @pl.loop(0, 2)
    def _(i):
        at = pl.ds(pl.multiple_of(i * 128, 128), 128)
        normed = stats(R.x1[at, :])[0].astype(BF16)
        R.n1[at, :] = normed
        for ref, weight in ((R.q1, R.wq), (R.k1, R.wk), (R.v1, R.wv)):
            ref[at, :] = dot(normed, weight[0]).astype(BF16)

    @pl.loop(0, 4)
    def _(w):
        at = pl.ds(pl.multiple_of(w * 64, 64), 64)
        z, z_heads = tile_ids(R.id1[at, :])
        probs = softmax_window(R.q1[at, :], by_heads(R.k1[at, :]), z, z_heads, R.bias[0])
        R.p1[at, :] = probs
        R.mix1[at, :] = dot(probs.astype(BF16), by_heads(R.v1[at, :])).astype(BF16)

    @pl.loop(0, 2)
    def _(i):
        at = pl.ds(pl.multiple_of(i * 128, 128), 128)
        middle = (R.x1[at, :] + dot(R.mix1[at, :], R.proj_w[0])).astype(BF16).astype(F32)
        R.mid1[at, :] = middle
        normed = stats(middle)[0].astype(BF16)
        R.m1[at, :] = normed
        act, slope = gelu_parts(dot(normed, R.inner_w[0]))
        act = act.astype(BF16)
        R.act1[at, :] = act
        R.slope1[at, :] = slope
        R.first[at, :] = (middle + dot_t(act, R.outer_w[0])).astype(BF16).astype(F32)


def exchange_forward(R, N):
    ext = R.ext
    for w in range(4):
        for r in range(8):
            t = w * 64 + r * 8
            piece = jnp.concatenate([R.first[t : t + 8, :], R.id1[t : t + 8, 0:64]], axis=1)
            ext[4 + r, 4 + w * 8 : 12 + w * 8, :] = piece
    for i, rim in enumerate((R.upper, R.lower)):
        for r in range(4):
            row = rim[r].astype(F32)
            R.rim[i, r] = jnp.concatenate([row, R.rim_id[i, r * 32 : r * 32 + 32, 0:64]], axis=1)
    for side, top in ((0, 4), (1, 8)):
        for r in range(4):
            R.pack[r * 32 : r * 32 + 32, :] = ext[top + r, 4:36, :]
        R.fs[side][...] = R.pack[0:128, :].astype(BF16)
    for side, left in ((2, 4), (3, 32)):
        for r in range(4):
            R.pack[r * 4 : r * 4 + 4, :] = R.rim[0, r, left - 4 : left, :]
            R.pack[48 + r * 4 : 52 + r * 4, :] = R.rim[1, r, left - 4 : left, :]
        for r in range(8):
            R.pack[16 + r * 4 : 20 + r * 4, :] = ext[4 + r, left : left + 4, :]
        R.fs[side][...] = R.pack[0:64, :].astype(BF16)
    for side, top, left in ((4, 4, 4), (5, 4, 32), (6, 8, 4), (7, 8, 32)):
        for r in range(4):
            R.pack[r * 4 : r * 4 + 4, :] = ext[top + r, left : left + 4, :]
        R.fs[side][...] = R.pack[0:16, :].astype(BF16)
    copies = []
    for side, (dr, dc) in enumerate(SIDES):
        copies.append(
            remote(
                R.fs[side], R.fr[side], R.fsend.at[side], R.frecv.at[side], N.near(dr, dc)
            )
        )
        copies[-1].start()
    for copy in copies:
        copy.wait()
    at_top = N.r == 0
    at_bottom = N.r == 15
    R.pack[...] = R.fr[1][...].astype(F32)
    for r in range(4):
        ext[r, 4:36, :] = jnp.where(at_top, R.rim[0, r], R.pack[r * 32 : r * 32 + 32, :])
    R.pack[...] = R.fr[0][...].astype(F32)
    for r in range(4):
        ext[12 + r, 4:36, :] = jnp.where(at_bottom, R.rim[1, r], R.pack[r * 32 : r * 32 + 32, :])
    for strip, above, below, left in ((3, 7, 5, 0), (2, 6, 4, 36)):
        R.pack[0:64, :] = R.fr[strip][...].astype(F32)
        R.pack[64:80, :] = R.fr[above][...].astype(F32)
        R.pack[80:96, :] = R.fr[below][...].astype(F32)
        for r in range(4):
            own = R.pack[r * 4 : r * 4 + 4, :]
            ext[r, left : left + 4, :] = jnp.where(at_top, own, R.pack[64 + r * 4 : 68 + r * 4, :])
            own = R.pack[48 + r * 4 : 52 + r * 4, :]
            ext[12 + r, left : left + 4, :] = jnp.where(at_bottom, own, R.pack[80 + r * 4 : 84 + r * 4, :])
        for r in range(8):
            ext[4 + r, left : left + 4, :] = R.pack[16 + r * 4 : 20 + r * 4, :]


def query_start(n):
    return n * 64 + (1 - n // 5) * 32


def forward_two(R):
    ext = R.ext
    for a in range(2):
        for b in range(5):
            for i in range(8):
                t = ((a * 5 + b) * 8 + i) * 8
                piece = ext[a * 8 + i, b * 8 : b * 8 + 8, :]
                R.x2[t : t + 8, :] = piece[:, 0:C]
                R.id2[t : t + 8, :] = jnp.broadcast_to(piece[:, C : C + 1], (8, 128))
    R.cot_ext[...] = jnp.zeros_like(R.cot_ext)
    for r in range(8):
        R.cot_ext[r, 4:36, :] = R.cot[r].astype(F32)
    for a in range(2):
        for b in range(5):
            for i in range(4):
                t = (a * 5 + b) * 32 + i * 8
                R.g2[t : t + 8, :] = R.cot_ext[a * 4 + i, b * 8 : b * 8 + 8, :]

    @pl.loop(0, 5)
    def _(i):
        at = pl.ds(pl.multiple_of(i * 128, 128), 128)
        normed = stats(R.x2[at, :])[0].astype(BF16)
        R.n2[at, :] = normed
        for ref, weight in ((R.k2, R.wk), (R.v2, R.wv)):
            ref[at, :] = dot(normed, weight[1]).astype(BF16)

    for n in range(10):
        start = query_start(n)
        R.nq2[n * 32 : n * 32 + 32, :] = R.n2[start : start + 32, :]
        R.xq2[n * 32 : n * 32 + 32, :] = R.x2[start : start + 32, :]
    R.q2[...] = dot(R.nq2[...], R.wq[1]).astype(BF16)

    @pl.loop(0, 10)
    def _(n):
        keys = pl.ds(pl.multiple_of(n * 64, 64), 64)
        queries = pl.ds(pl.multiple_of(n * 32, 32), 32)
        half = pl.ds(pl.multiple_of((1 - n // 5) * 32, 32), 32)
        within = pl.ds(pl.multiple_of(query_start(n), 32), 32)
        z_heads = tile_ids(R.id2[keys, :])[1]
        z = tile_ids(R.id2[within, :])[0]
        probs = softmax_window(R.q2[queries, :], by_heads(R.k2[keys, :]), z, z_heads, R.bias[1, half, :])
        R.p2[queries, :] = probs
        R.mix2[queries, :] = dot(probs.astype(BF16), by_heads(R.v2[keys, :])).astype(BF16)

    @pl.loop(0, 2)
    def _(i):
        at = pl.ds(pl.multiple_of(i * 160, 32), 160)
        middle = (R.xq2[at, :] + dot(R.mix2[at, :], R.proj_w[1])).astype(BF16).astype(F32)
        normed = stats(middle)[0].astype(BF16)
        R.m2[at, :] = normed
        act, slope = gelu_parts(dot(normed, R.inner_w[1]))
        R.act2[at, :] = act.astype(BF16)
        grad_out = R.g2[at, :]
        grad_pre = (slope * dot(grad_out.astype(BF16), R.outer_w[1])).astype(BF16)
        R.pre2[at, :] = grad_pre
        grad_mid = (grad_out + norm_back(middle, dot_t(grad_pre, R.inner_w[1]))).astype(BF16)
        R.gm2[at, :] = grad_mid
        R.e2[at, :] = dot_t(grad_mid, R.proj_w[1]).astype(BF16)


def window_back(probs, e, q, k_heads, v_heads):
    grad_probs = dot_t(e, v_heads)
    grad_scores = probs * (grad_probs - head_reduce(grad_probs * probs, jnp.sum, 0.0))
    low = grad_scores.astype(BF16)
    grad_q = (dot(low, k_heads) * SCALE).astype(BF16)
    grad_k = (gather_heads(t_dot(low, q)) * SCALE).astype(BF16)
    grad_v = gather_heads(t_dot(probs.astype(BF16), e)).astype(BF16)
    return grad_scores, grad_q, grad_k, grad_v


def attend_back_two(R):
    R.gb[1] = jnp.zeros((64, 384), F32)

    @pl.loop(0, 10)
    def _(n):
        keys = pl.ds(pl.multiple_of(n * 64, 64), 64)
        queries = pl.ds(pl.multiple_of(n * 32, 32), 32)
        half = pl.ds(pl.multiple_of((1 - n // 5) * 32, 32), 32)
        grad_scores, grad_q, grad_k, grad_v = window_back(
            R.p2[queries, :],
            R.e2[queries, :],
            R.q2[queries, :],
            by_heads(R.k2[keys, :]),
            by_heads(R.v2[keys, :]),
        )
        R.gb[1, half, :] = R.gb[1, half, :] + grad_scores
        R.dq2[queries, :] = grad_q
        R.dk2[keys, :] = grad_k
        R.dv2[keys, :] = grad_v

    R.dnq2[...] = dot_t(R.dq2[...], R.wq[1])

    @pl.loop(0, 5)
    def _(i):
        at = pl.ds(pl.multiple_of(i * 128, 128), 128)
        R.dn2[at, :] = dot_t(R.dk2[at, :], R.wk[1]) + dot_t(R.dv2[at, :], R.wv[1])

    @pl.loop(0, 10)
    def _(n):
        queries = pl.ds(pl.multiple_of(n * 32, 32), 32)
        within = pl.ds(pl.multiple_of(query_start(n), 32), 32)
        R.dn2[within, :] = R.dn2[within, :] + R.dnq2[queries, :]

    @pl.loop(0, 5)
    def _(i):
        at = pl.ds(pl.multiple_of(i * 128, 128), 128)
        R.dn2[at, :] = norm_back(R.x2[at, :], R.dn2[at, :])

    @pl.loop(0, 10)
    def _(n):
        queries = pl.ds(pl.multiple_of(n * 32, 32), 32)
        within = pl.ds(pl.multiple_of(query_start(n), 32), 32)
        R.dn2[within, :] = R.dn2[within, :] + R.gm2[queries, :].astype(F32)


def back_copy(R, N, side):
    dr, dc = SIDES[side]
    return remote(R.bs[side], R.br[side], R.bsend.at[side], R.brecv.at[side], N.near(dr, dc))


def send_back(R, N):
    ext = R.dext
    for a in range(2):
        for b in range(5):
            for i in range(8):
                t = ((a * 5 + b) * 8 + i) * 8
                ext[a * 8 + i, b * 8 : b * 8 + 8, :] = R.dn2[t : t + 8, :]
    pack = R.pack
    for side, top in ((0, 0), (1, 12)):
        for r in range(4):
            pack[r * 32 : r * 32 + 32, 0:C] = ext[top + r, 4:36, :]
        R.bs[side][...] = pack[0:128, 0:C].astype(BF16)
    for side, left in ((2, 0), (3, 36)):
        for r in range(8):
            pack[r * 4 : r * 4 + 4, 0:C] = ext[4 + r, left : left + 4, :]
        R.bs[side][...] = pack[0:32, 0:C].astype(BF16)
    for side, top, left in ((4, 0, 0), (5, 0, 36), (6, 12, 0), (7, 12, 36)):
        for r in range(4):
            pack[r * 4 : r * 4 + 4, 0:C] = ext[top + r, left : left + 4, :]
        R.bs[side][...] = pack[0:16, 0:C].astype(BF16)
    for side in range(8):
        back_copy(R, N, side).start()


def receive_back(R, N):
    for side in range(8):
        back_copy(R, N, side).wait()
    ext, pack = R.dext, R.pack
    above = jnp.where(N.r == 0, 0.0, 1.0).astype(F32)
    below = jnp.where(N.r == 15, 0.0, 1.0).astype(F32)
    pack[...] = jnp.zeros_like(pack)
    for side, top, left, rows, cols, keep in (
        (1, 4, 4, 4, 32, above),
        (0, 8, 4, 4, 32, below),
        (3, 4, 4, 8, 4, None),
        (2, 4, 32, 8, 4, None),
        (7, 4, 4, 4, 4, above),
        (6, 4, 32, 4, 4, above),
        (5, 8, 4, 4, 4, below),
        (4, 8, 32, 4, 4, below),
    ):
        received = R.br[side][...].astype(F32)
        if keep is not None:
            received = jnp.where(keep > 0.5, received, 0.0)
        pack[0 : BACK_ROWS[side], 0:C] = received
        for r in range(rows):
            ext[top + r, left : left + cols, :] = (
                ext[top + r, left : left + cols, :] + pack[r * cols : r * cols + cols, 0:C]
            )
    for w in range(4):
        for r in range(8):
            t = w * 64 + r * 8
            R.g1[t : t + 8, :] = ext[4 + r, 4 + w * 8 : 12 + w * 8, :]


def channel_back_one(R):
    @pl.loop(0, 2)
    def _(i):
        at = pl.ds(pl.multiple_of(i * 128, 128), 128)
        grad_out = R.g1[at, :].astype(BF16)
        R.gf1[at, :] = grad_out
        grad_pre = (R.slope1[at, :] * dot(grad_out, R.outer_w[0])).astype(BF16)
        R.pre1[at, :] = grad_pre
        back = norm_back(R.mid1[at, :], dot_t(grad_pre, R.inner_w[0]))
        grad_mid = (grad_out.astype(F32) + back).astype(BF16)
        R.gm1[at, :] = grad_mid
        R.e1[at, :] = dot_t(grad_mid, R.proj_w[0]).astype(BF16)


def attend_back_one(R):
    R.gb[0] = jnp.zeros((64, 384), F32)

    @pl.loop(0, 4)
    def _(w):
        at = pl.ds(pl.multiple_of(w * 64, 64), 64)
        grad_scores, grad_q, grad_k, grad_v = window_back(
            R.p1[at, :],
            R.e1[at, :],
            R.q1[at, :],
            by_heads(R.k1[at, :]),
            by_heads(R.v1[at, :]),
        )
        R.gb[0] = R.gb[0] + grad_scores
        R.dq1[at, :] = grad_q
        R.dk1[at, :] = grad_k
        R.dv1[at, :] = grad_v


def finish_one(R):
    @pl.loop(0, 2)
    def _(i):
        at = pl.ds(pl.multiple_of(i * 128, 128), 128)
        grad = dot_t(R.dq1[at, :], R.wq[0])
        grad = grad + dot_t(R.dk1[at, :], R.wk[0]) + dot_t(R.dv1[at, :], R.wv[0])
        R.x1[at, :] = R.gm1[at, :].astype(F32) + norm_back(R.x1[at, :], grad)

    for r in range(8):
        row = [R.x1[w * 64 + r * 8 : w * 64 + r * 8 + 8, :] for w in range(4)]
        R.token_grad[r] = jnp.concatenate(row, axis=0).astype(BF16)


def grads_of(R, N, b):
    pick = R.pick_ch[...]
    normed = dot((R.n1, R.n2)[b][...], pick).astype(BF16)
    query_normed = dot(R.nq2[...], pick).astype(BF16) if b else normed
    R.t_qkv[0:C, :] = t_dot((R.dq1, R.dq2)[b][...], query_normed)
    R.t_qkv[C : 2 * C, :] = t_dot((R.dk1, R.dk2)[b][...], normed)
    R.t_qkv[2 * C : 3 * C, :] = t_dot((R.dv1, R.dv2)[b][...], normed)
    R.t_proj[...] = t_dot((R.gm1, R.gm2)[b][...], dot((R.mix1, R.mix2)[b][...], pick).astype(BF16))
    R.t_inner[...] = t_dot((R.pre1, R.pre2)[b][...], dot((R.m1, R.m2)[b][...], pick).astype(BF16))
    grad_out = R.g2[...].astype(BF16) if b else R.gf1[...]
    for s in range(4):
        act = dot((R.act1, R.act2)[b][...], R.pick_hid[:, s * 256 : s * 256 + 256]).astype(BF16)
        R.t_outer[s] = t_dot(grad_out, act)

    @pl.loop(0, 8)
    def _(y):
        def part(ref, width):
            return ref[pl.ds(pl.multiple_of(y * width, 8), width), :]

        stacked = [part(R.t_qkv, 72), part(R.t_proj, 24), part(R.t_inner, 96)]
        stacked += [part(R.t_outer.at[s], 24) for s in range(4)]
        chunks = dot(R.cut[...], jnp.concatenate(stacked, axis=0).astype(BF16)).astype(BF16)
        for q in range(4):
            for x_lo in range(2):
                R.ga[b, q % 2, q // 2 * 2 + x_lo, y] = chunks[
                    q * CHUNK : q * CHUNK + CHUNK, x_lo * 128 : x_lo * 128 + 128
                ]

    R.tab[b * 8 : b * 8 + 8, :] = fold_bias(R.gb.at[b], R.offsets)


def core_copy(R, N, b):
    return remote(
        R.ga.at[b, 1 - N.core], R.ra.at[b], R.asend.at[b], R.arecv.at[b], N.partner()
    )


def start_core(R, N, b):
    core_copy(R, N, b).start()
    if b == 0:
        R.ta[...] = R.tab[...].astype(BF16)
        table_copy(R, N).start()


def table_copy(R, N):
    return remote(R.ta, R.rta, R.tsend.at[0], R.trecv.at[0], N.partner())


def spread_copies(R, send, recv, src, dst, base, me, n, device):
    def sending(other, d):
        return remote(src(other), dst(me), send.at[base + d], recv.at[base + me], device(other))

    def arriving(other, d):
        return remote(src(other), dst(other), send.at[base + d], recv.at[base + other], device(other))

    return [(functools.partial(sending, (me + d) % n, d), functools.partial(arriving, (me + d) % n, d)) for d in range(1, n)]


def x_copies(R, N, b):
    return spread_copies(
        R, R.xsend, R.xrecv, lambda o: R.hb.at[b, o], lambda s: R.rb.at[b, s], b * 4, N.x, 4, N.at_x
    )


def y_copies(R, N, b):
    return spread_copies(
        R, R.ysend, R.yrecv, lambda o: R.hc.at[b, o], lambda s: R.rc.at[b, s], b * 8, N.y, 8, N.at_y
    )


def z_copies(R, N, b):
    return spread_copies(
        R, R.zsend, R.zrecv, lambda o: R.hd.at[b, o], lambda s: R.rd.at[b, s], b * 8, N.z, 8, N.at_z
    )


def table_copies(R, N, stage):
    me, n, device = ((N.x, 4, N.at_x), (N.y, 8, N.at_y), (N.z, 8, N.at_z))[stage]
    base = stage * 8
    src, dst = R.table_out[stage], R.table_in[stage]
    return spread_copies(
        R, R.tbsend, R.tbrecv, lambda o: src, lambda s: dst.at[s], base, me, n, device
    )


def go(copies):
    for sending, _ in copies:
        sending().start()


def settle(copies):
    for sending, arriving in copies:
        sending().wait_send()
        arriving().wait_recv()


def table_sum(R, N, stage):
    settle(table_copies(R, N, stage))
    n = 8 if stage else 4
    received = R.table_in[stage]
    total = received[0].astype(F32)
    for s in range(1, n):
        total = total + received[s].astype(F32)
    return total


def table_send(R, N, stage, total):
    me = (N.x, N.y, N.z)[stage]
    low = total.astype(BF16)
    R.table_out[stage][...] = low
    R.table_in[stage][me] = low
    go(table_copies(R, N, stage))


def start_x(R, N, b):
    core_copy(R, N, b).wait()

    @pl.loop(0, 4)
    def _(x):
        for y in range(8):
            total = R.ga[b, N.core, x, y].astype(F32) + R.ra[b, x, y].astype(F32)
            R.hb[b, x, y] = total.astype(BF16)

    go(x_copies(R, N, b))
    if b == 0:
        table_copy(R, N).wait()
        table_send(R, N, 0, R.ta[...].astype(F32) + R.rta[...].astype(F32))


def start_y(R, N, b):
    settle(x_copies(R, N, b))

    @pl.loop(0, 8)
    def _(y):
        total = R.hb[b, N.x, y].astype(F32)
        for d in range(1, 4):
            total = total + R.rb[b, (N.x + d) % 4, y].astype(F32)
        R.hc[b, y] = total.astype(BF16)

    go(y_copies(R, N, b))
    if b == 0:
        table_send(R, N, 1, table_sum(R, N, 0))


def start_z(R, N, b):
    settle(y_copies(R, N, b))
    total = R.hc[b, N.y].astype(F32)
    for d in range(1, 8):
        total = total + R.rc[b, (N.y + d) % 8].astype(F32)
    R.turn[...] = jnp.concatenate([total, jnp.zeros((128 - CHUNK, 128), F32)], axis=0).T
    for z in range(8):
        R.hd[b, z] = R.turn[z * 12 : z * 12 + 16, :].astype(BF16)
    go(z_copies(R, N, b))
    if b == 0:
        table_send(R, N, 2, table_sum(R, N, 1))


def finish_z(R, N, b):
    settle(z_copies(R, N, b))
    total = R.hd[b, N.z].astype(F32)
    for d in range(1, 8):
        total = total + R.rd[b, (N.z + d) % 8].astype(F32)
    total = total * (1.0 / 512.0)
    R.qkv_grad[:, b, :] = total[0:12, 0:18]
    R.inner_grad[:, b, :] = total[0:12, 24:48]
    turned = jnp.concatenate([total, jnp.zeros((112, 128), F32)], axis=0).T
    R.proj_grad[:, b, :] = turned[18:24, 0:12]
    outer = [turned[48 + 6 * s : 54 + 6 * s, 0:12] for s in range(4)]
    R.outer_grad[:, b, :] = jnp.concatenate(outer, axis=1)
    if b == 0:
        R.tab[...] = table_sum(R, N, 2) * (1.0 / 512.0)


def finish_table(R):
    for b in range(2):
        R.table_grad[:, b, :] = R.tab[b * 8 : b * 8 + 6, 0:225]


def scratch():
    def f(*shape):
        return pltpu.VMEM(shape, F32)

    def h(*shape):
        return pltpu.VMEM(shape, BF16)

    def semaphores(count):
        return pltpu.SemaphoreType.DMA((count,))

    out = dict(wq=h(2, C, C), wk=h(2, C, C), wv=h(2, C, C), bias=f(2, 64, 384))
    out.update(x1=f(256, C), id1=f(256, 128), rim_id=f(2, 128, 128), rim=f(2, 4, 32, CW))
    out.update(pick_hid=h(HID, 1024), pick_ch=h(C, 256), cut=h(4 * CHUNK, 288))
    out.update(n1=h(256, C), q1=h(256, C), k1=h(256, C), v1=h(256, C), mix1=h(256, C), m1=h(256, C))
    out.update(gf1=h(256, C), gm1=h(256, C), e1=h(256, C), dq1=h(256, C), dk1=h(256, C), dv1=h(256, C))
    out.update(p1=f(256, 384), mid1=f(256, C), first=f(256, C), g1=f(256, C))
    out.update(act1=h(256, HID), slope1=f(256, HID), pre1=h(256, HID))
    out.update(ext=f(16, 40, CW), dext=f(16, 40, C), cot_ext=f(8, 40, C), pack=f(128, CW))
    out.update(x2=f(640, C), id2=f(640, 128), dn2=f(640, C))
    out.update(n2=h(640, C), k2=h(640, C), v2=h(640, C), dk2=h(640, C), dv2=h(640, C))
    out.update(nq2=h(320, C), q2=h(320, C), mix2=h(320, C), m2=h(320, C), gm2=h(320, C), e2=h(320, C), dq2=h(320, C))
    out.update(xq2=f(320, C), g2=f(320, C), dnq2=f(320, C), p2=f(320, 384))
    out.update(act2=h(320, HID), pre2=h(320, HID), gb=f(2, 64, 384))
    out.update(t_qkv=f(576, 256), t_proj=f(C, 256), t_inner=f(HID, 256), t_outer=f(4, C, 256))
    out.update(offsets=h(WIN, 256, 128), tab=f(16, 256), turn=f(128, 128))
    out.update(fs=[h(n, CW) for n in SIDE_ROWS], fr=[h(n, CW) for n in SIDE_ROWS])
    out.update(bs=[h(n, C) for n in BACK_ROWS], br=[h(n, C) for n in BACK_ROWS])
    out.update(ga=h(2, 2, 4, 8, CHUNK, 128), ra=h(2, 4, 8, CHUNK, 128))
    out.update(hb=h(2, 4, 8, CHUNK, 128), rb=h(2, 4, 8, CHUNK, 128))
    out.update(hc=h(2, 8, CHUNK, 128), rc=h(2, 8, CHUNK, 128), hd=h(2, 8, 16, 128), rd=h(2, 8, 16, 128))
    out.update(ta=h(16, 256), rta=h(16, 256), table_out=[h(16, 256)] * 3)
    out.update(table_in=[h(4, 16, 256), h(8, 16, 256), h(8, 16, 256)])
    out.update(fsend=semaphores(8), frecv=semaphores(8), bsend=semaphores(8), brecv=semaphores(8))
    out.update(asend=semaphores(2), arecv=semaphores(2), tsend=semaphores(1), trecv=semaphores(1))
    out.update(xsend=semaphores(8), xrecv=semaphores(8), ysend=semaphores(16), yrecv=semaphores(16))
    out.update(zsend=semaphores(16), zrecv=semaphores(16), tbsend=semaphores(24), tbrecv=semaphores(24))
    return out


SHAPES, STRUCTURE = jax.tree.flatten(scratch(), is_leaf=lambda x: not isinstance(x, (dict, list)))
COUNT = 18


def local(
    tokens,
    region_ids,
    upper_rim,
    upper_ids,
    lower_rim,
    lower_ids,
    cotangent,
    qkv_weight,
    proj_weight,
    inner_weight,
    outer_weight,
    bias_table,
):
    out = pl.pallas_call(
        body,
        out_shape=(
            jax.ShapeDtypeStruct((8, 32, C), BF16),
            jax.ShapeDtypeStruct((12, 2, 18), F32),
            jax.ShapeDtypeStruct((6, 2, 12), F32),
            jax.ShapeDtypeStruct((12, 2, 24), F32),
            jax.ShapeDtypeStruct((6, 2, 48), F32),
            jax.ShapeDtypeStruct((6, 2, 225), F32),
        ),
        in_specs=[pl.BlockSpec(memory_space=pltpu.VMEM)] * 12,
        out_specs=[pl.BlockSpec(memory_space=pltpu.VMEM)] * 6,
        scratch_shapes=SHAPES,
        compiler_params=pltpu.CompilerParams(
            collective_id=0, has_side_effects=True, vmem_limit_bytes=60 * 1024 * 1024
        ),
        name="blocks",
    )(
        tokens,
        region_ids,
        upper_rim,
        upper_ids,
        lower_rim,
        lower_ids,
        cotangent,
        qkv_weight,
        proj_weight,
        inner_weight,
        outer_weight.transpose(0, 2, 1),
        bias_table.transpose(2, 0, 1),
    )
    orders = ((1, 0, 2), (1, 2, 0), (1, 0, 2), (1, 2, 0), (1, 2, 0))
    return (out[0], *(part.transpose(order) for part, order in zip(out[1:], orders)))


def solution(mesh):
    return jax.shard_map(
        local,
        mesh=mesh,
        in_specs=(
            P("rows", "cols", None),
            P("rows", "cols"),
            P(None, "cols", None),
            P(None, "cols"),
            P(None, "cols", None),
            P(None, "cols"),
            P("rows", "cols", None),
            P(),
            P(),
            P(),
            P(),
            P(),
        ),
        out_specs=(
            P("rows", "cols", None),
            P(None, "rows", "cols"),
            P(None, "rows", "cols"),
            P(None, "rows", "cols"),
            P(None, "rows", "cols"),
            P(),
        ),
        check_vma=False,
    )
```

```python
import functools
import math
import types

import jax
import jax.numpy as jnp
from jax import lax
from jax.experimental import pallas as pl
from jax.experimental.pallas import tpu as pltpu
from jax.sharding import PartitionSpec as P

C = 192
HEADS = 6
HD = 32
HID = 768
WIN = 8
HALF = 4
EPS = 1e-05
MASKED = -1000000000.0
SCALE = HD**-0.5
CW = 256
CHUNK = 80
F32 = jnp.float32
BF16 = jnp.bfloat16
MESH = pl.DeviceIdType.MESH


def dot(a, b):
    return lax.dot_general(a, b, (((1,), (0,)), ((), ())), preferred_element_type=F32)


def dot_t(a, b):
    return lax.dot_general(a, b, (((1,), (1,)), ((), ())), preferred_element_type=F32)


def t_dot(a, b):
    return lax.dot_general(a, b, (((0,), (0,)), ((), ())), preferred_element_type=F32)


def iota(shape, dim):
    return lax.broadcasted_iota(jnp.int32, shape, dim)


def stats(values):
    center = jnp.sum(values, axis=-1, keepdims=True) * (1.0 / C)
    shifted = values - center
    spread = jnp.sum(shifted * shifted, axis=-1, keepdims=True) * (1.0 / C)
    inverse = lax.rsqrt(spread + EPS)
    return shifted * inverse, inverse


def norm_back(values, grad):
    hat, inverse = stats(values)
    mean_grad = jnp.sum(grad, axis=-1, keepdims=True) * (1.0 / C)
    mean_dot = jnp.sum(grad * hat, axis=-1, keepdims=True) * (1.0 / C)
    return inverse * (grad - mean_grad - hat * mean_dot)


def by_heads(values):
    lane_head = iota(values.shape, 1) // HD
    zero = jnp.zeros_like(values)
    return jnp.concatenate([jnp.where(lane_head == h, values, zero) for h in range(HEADS)], axis=0)


def gather_heads(stacked):
    lane_head = iota((64, C), 1) // HD
    total = jnp.zeros((64, C), F32)
    for h in range(HEADS):
        total = jnp.where(lane_head == h, stacked[h * 64 : h * 64 + 64], total)
    return total


def head_reduce(scores, reduce, fill):
    pieces = []
    for pair in range(3):
        part = scores[:, pair * 128 : pair * 128 + 128]
        first = iota(part.shape, 1) < 64
        low = reduce(jnp.where(first, part, fill), axis=-1, keepdims=True)
        high = reduce(jnp.where(first, fill, part), axis=-1, keepdims=True)
        pieces.append(jnp.where(first, low, high))
    return jnp.concatenate(pieces, axis=1)


def softmax_window(q, k_heads, z_q, z_heads, bias):
    scores = dot_t(q, k_heads) * SCALE + bias
    scores = jnp.where(dot_t(z_q, z_heads) > 0.5, scores, MASKED)
    exponent = jnp.exp(scores - head_reduce(scores, jnp.max, -jnp.inf))
    return exponent / head_reduce(exponent, jnp.sum, 0.0)


def tile_ids(ids):
    z = (iota(ids.shape, 1).astype(F32) == ids).astype(BF16)
    return z, jnp.concatenate([z] * HEADS, axis=0)


def gelu_parts(pre):
    cdf = 0.5 * (1.0 + lax.erf(pre * (1.0 / math.sqrt(2.0))))
    slope = cdf + pre * (jnp.exp(-0.5 * pre * pre) * (1.0 / math.sqrt(2.0 * math.pi)))
    return pre * cdf, slope


def split(values):
    high = values.astype(BF16)
    rest = values - high.astype(F32)
    middle = rest.astype(BF16)
    low = (rest - middle.astype(F32)).astype(BF16)
    return jnp.concatenate([high, middle, low], axis=0)


def joined(pieces):
    n = pieces.shape[0] // 3
    return pieces[0:n] + pieces[n : 2 * n] + pieces[2 * n :]


def offset_onehots(out_ref):
    lane = iota((1, 128), 1)
    row = iota((256, 128), 0)
    for ci in range(WIN):
        offset = jnp.where(lane < 120, (14 - lane // 8) * 15 + (ci - lane % 8 + 7), -1)
        out_ref[ci] = (row == offset).astype(BF16)


def spread_bias(R):
    R.tab[...] = jnp.zeros((16, 256), F32)
    for b in range(2):
        R.tab[b * 8 : b * 8 + 6, 0:225] = R.table[:, b, :]
    pieces = split(R.tab[...])
    per_column = [joined(dot(pieces, R.offsets[ci])) for ci in range(WIN)]
    first = iota((8, 128), 1) < 64
    for b in range(2):
        per_head = [
            jnp.concatenate([per_column[ci][b * 8 + h : b * 8 + h + 1] for ci in range(WIN)], axis=0)
            for h in range(HEADS)
        ]
        for ri in range(WIN):
            shift = (7 - ri) * 8
            for pair in range(3):
                low = pltpu.roll(per_head[2 * pair], (128 - shift) % 128, 1)
                high = pltpu.roll(per_head[2 * pair + 1], (64 - shift) % 128, 1)
                R.bias[b, ri * 8 : ri * 8 + 8, pair * 128 : pair * 128 + 128] = jnp.where(first, low, high)


def fold_bias(grad_ref, offsets):
    first = iota((8, 128), 1) < 64
    per_head = [jnp.zeros((8, 128), F32) for _ in range(HEADS)]
    for ri in range(WIN):
        shift = (7 - ri) * 8
        for pair in range(3):
            part = grad_ref[ri * 8 : ri * 8 + 8, pair * 128 : pair * 128 + 128]
            low = pltpu.roll(jnp.where(first, part, 0.0), shift % 128, 1)
            high = pltpu.roll(jnp.where(first, 0.0, part), (shift + 64) % 128, 1)
            per_head[2 * pair] = per_head[2 * pair] + low
            per_head[2 * pair + 1] = per_head[2 * pair + 1] + high
    total = jnp.zeros((8, 256), F32)
    for ci in range(WIN):
        rows = jnp.concatenate([per_head[h][ci : ci + 1] for h in range(HEADS)] + [jnp.zeros((2, 128), F32)], axis=0)
        total = total + joined(dot_t(split(rows), offsets[ci]))
    return total


def place():
    r = lax.axis_index("rows")
    c = lax.axis_index("cols")
    return r, c


class Net:
    def __init__(self):
        r, c = place()
        self.r, self.c = r, c
        self.x_lo, self.z = r // 8, r % 8
        self.y, self.x_hi, self.core = c // 4, (c // 2) % 2, c % 2
        self.x = self.x_hi * 2 + self.x_lo

    def near(self, dr, dc):
        return ((self.r + dr + 16) % 16, (self.c + dc + 32) % 32)

    def partner(self):
        return (self.r, self.c + 1 - 2 * self.core)

    def at_x(self, x):
        return ((x % 2) * 8 + self.z, self.y * 4 + (x // 2) * 2 + self.core)

    def at_y(self, y):
        return (self.r, y * 4 + self.x_hi * 2 + self.core)

    def at_z(self, z):
        return (self.x_lo * 8 + z, self.c)

    def everyone(self):
        peers = [self.near(dr, dc) for dr, dc in SIDES] + [self.partner()]
        peers += [self.at_x((self.x + d) % 4) for d in range(1, 4)]
        peers += [self.at_y((self.y + d) % 8) for d in range(1, 8)]
        peers += [self.at_z((self.z + d) % 8) for d in range(1, 8)]
        return peers


SIDES = ((-1, 0), (1, 0), (0, -1), (0, 1), (-1, -1), (-1, 1), (1, -1), (1, 1))
SIDE_ROWS = (128, 128, 64, 64, 16, 16, 16, 16)
BACK_ROWS = (128, 128, 32, 32, 16, 16, 16, 16)


def remote(src, dst, send, recv, device):
    return pltpu.make_async_remote_copy(
        src_ref=src, dst_ref=dst, send_sem=send, recv_sem=recv, device_id=device, device_id_type=MESH
    )


def body(*refs):
    R = types.SimpleNamespace(**jax.tree.unflatten(STRUCTURE, refs[COUNT:]))
    R.tokens, R.ids, R.upper, R.upper_ids, R.lower, R.lower_ids, R.cot = refs[:7]
    R.qkv_w, R.proj_w, R.inner_w, R.outer_w, R.table, R.token_grad, R.totals = refs[7:14]
    R.table_total = refs[14]
    N = Net()

    barrier = pltpu.get_barrier_semaphore()
    peers = N.everyone()
    for peer in peers:
        pl.semaphore_signal(barrier, inc=1, device_id=peer, device_id_type=MESH)

    setup(R)
    forward_one(R)
    pl.semaphore_wait(barrier, len(peers))
    exchange_forward(R, N)
    forward_two(R)
    attend_back_two(R)
    send_back(R, N)
    grads_of(R, 1)
    start_core(R, N, 1)
    table_of(R, 1)
    receive_back(R, N)
    channel_back_one(R)
    start_x(R, N, 1)
    attend_back_one(R)
    start_y(R, N, 1)
    grads_of(R, 0)
    start_core(R, N, 0)
    table_of(R, 0)
    start_table(R, N)
    finish_one(R)
    start_z(R, N, 1)
    start_x(R, N, 0)
    finish_z(R, N, 1)
    start_y(R, N, 0)
    start_z(R, N, 0)
    finish_z(R, N, 0)


def select_column(rows, order, ids):
    n = ids.shape[0]
    row_of, col_of = order
    pick = (iota((rows, n), 1) == row_of(iota((rows, n), 0))).astype(BF16)
    spread = dot(pick, ids.astype(F32).astype(BF16))
    keep = iota((rows, 32), 1) == col_of(iota((rows, 32), 0))
    column = jnp.sum(jnp.where(keep, spread, 0.0), axis=-1, keepdims=True)
    return jnp.broadcast_to(column, (rows, 128))


def setup(R):
    offset_onehots(R.offsets)
    spread_bias(R)
    for i, ref in enumerate((R.wq, R.wk, R.wv)):
        ref[0] = R.qkv_w[0][:, i * C : i * C + C]
    for r in range(8):
        row = R.tokens[r].astype(F32)
        for w in range(4):
            R.x1[w * 64 + r * 8 : w * 64 + r * 8 + 8, :] = row[w * 8 : w * 8 + 8]
    by_window = (lambda t: (t // 8) % 8, lambda t: (t // 64) * 8 + t % 8)
    by_row = (lambda t: t // 32, lambda t: t % 32)
    R.id1[...] = select_column(256, by_window, R.ids[...])
    R.rim_id[0] = select_column(128, by_row, R.upper_ids[...])
    R.rim_id[1] = select_column(128, by_row, R.lower_ids[...])


def setup_later(R):
    for i, ref in enumerate((R.wq, R.wk, R.wv)):
        ref[1] = R.qkv_w[1][:, i * C : i * C + C]
    R.cot_ext[...] = jnp.zeros_like(R.cot_ext)
    for r in range(8):
        R.cot_ext[r, 4:36, :] = R.cot[r].astype(F32)
    for a in range(2):
        for b in range(5):
            for i in range(4):
                t = (a * 5 + b) * 32 + i * 8
                R.g2[t : t + 8, :] = R.cot_ext[a * 4 + i, b * 8 : b * 8 + 8, :]
    lane = iota((1, 1024), 1)
    inside = lane % 128
    row = (lane // 128 % 2 * 8 + inside // 12) * 48 + lane // 256 * 12 + inside % 12
    row = jnp.where(inside < 96, row, -1)
    R.pick_hid[...] = (iota((HID, 1024), 0) == row).astype(BF16)
    lane = iota((1, 256), 1)
    inside = lane % 128
    row = jnp.where(inside < 96, lane // 128 * 96 + inside, -1)
    R.pick_ch[...] = (iota((C, 256), 0) == row).astype(BF16)
    out = iota((4 * CHUNK, 1), 0)
    q, k = out // CHUNK, out % CHUNK
    hid = (k - 48) // 6
    col = jnp.where(
        k < 18,
        18 * q + k,
        jnp.where(
            k < 24,
            72 + 6 * q + k - 18,
            jnp.where(k < 48, 96 + 24 * q + k - 24, 192 + 24 * hid + 6 * q + (k - 48 - 6 * hid)),
        ),
    )
    col = jnp.where(k < 72, col, -1)
    R.cut[...] = (iota((4 * CHUNK, 288), 1) == col).astype(BF16)


def forward_one(R):
    @pl.loop(0, 2)
    def _(i):
        at = pl.ds(pl.multiple_of(i * 128, 128), 128)
        normed = stats(R.x1[at, :])[0].astype(BF16)
        R.n1[at, :] = normed
        for ref, weight in ((R.q1, R.wq), (R.k1, R.wk), (R.v1, R.wv)):
            ref[at, :] = dot(normed, weight[0]).astype(BF16)

    @pl.loop(0, 2)
    def _(pair):
        done = []
        for w in (pair * 2, pair * 2 + 1):
            at = pl.ds(pl.multiple_of(w * 64, 64), 64)
            z, z_heads = tile_ids(R.id1[at, :])
            probs = softmax_window(R.q1[at, :], by_heads(R.k1[at, :]), z, z_heads, R.bias[0])
            mix = dot(probs.astype(BF16), by_heads(R.v1[at, :])).astype(BF16)
            done.append((at, probs, mix))
        for at, probs, mix in done:
            R.p1[at, :] = probs
            R.mix1[at, :] = mix

    @pl.loop(0, 2)
    def _(i):
        at = pl.ds(pl.multiple_of(i * 128, 128), 128)
        middle = (R.x1[at, :] + dot(R.mix1[at, :], R.proj_w[0])).astype(BF16).astype(F32)
        R.mid1[at, :] = middle
        normed = stats(middle)[0].astype(BF16)
        R.m1[at, :] = normed
        act, slope = gelu_parts(dot(normed, R.inner_w[0]))
        act = act.astype(BF16)
        R.act1[at, :] = act
        R.slope1[at, :] = slope
        R.first[at, :] = (middle + dot_t(act, R.outer_w[0])).astype(BF16).astype(F32)


def exchange_forward(R, N):
    ext = R.ext
    for w in range(4):
        for r in range(8):
            t = w * 64 + r * 8
            piece = jnp.concatenate([R.first[t : t + 8, :], R.id1[t : t + 8, 0:64]], axis=1)
            ext[4 + r, 4 + w * 8 : 12 + w * 8, :] = piece
    for i, rim in enumerate((R.upper, R.lower)):
        for r in range(4):
            row = rim[r].astype(F32)
            R.rim[i, r] = jnp.concatenate([row, R.rim_id[i, r * 32 : r * 32 + 32, 0:64]], axis=1)
    for side, top in ((0, 4), (1, 8)):
        for r in range(4):
            R.pack[r * 32 : r * 32 + 32, :] = ext[top + r, 4:36, :]
        R.fs[side][...] = R.pack[0:128, :].astype(BF16)
    for side, left in ((2, 4), (3, 32)):
        for r in range(4):
            R.pack[r * 4 : r * 4 + 4, :] = R.rim[0, r, left - 4 : left, :]
            R.pack[48 + r * 4 : 52 + r * 4, :] = R.rim[1, r, left - 4 : left, :]
        for r in range(8):
            R.pack[16 + r * 4 : 20 + r * 4, :] = ext[4 + r, left : left + 4, :]
        R.fs[side][...] = R.pack[0:64, :].astype(BF16)
    for side, top, left in ((4, 4, 4), (5, 4, 32), (6, 8, 4), (7, 8, 32)):
        for r in range(4):
            R.pack[r * 4 : r * 4 + 4, :] = ext[top + r, left : left + 4, :]
        R.fs[side][...] = R.pack[0:16, :].astype(BF16)
    copies = []
    for side, (dr, dc) in enumerate(SIDES):
        copies.append(
            remote(
                R.fs[side], R.fr[side], R.fsend.at[side], R.frecv.at[side], N.near(dr, dc)
            )
        )
        copies[-1].start()
    setup_later(R)
    for copy in copies:
        copy.wait()
    at_top = N.r == 0
    at_bottom = N.r == 15
    R.pack[...] = R.fr[1][...].astype(F32)
    for r in range(4):
        ext[r, 4:36, :] = jnp.where(at_top, R.rim[0, r], R.pack[r * 32 : r * 32 + 32, :])
    R.pack[...] = R.fr[0][...].astype(F32)
    for r in range(4):
        ext[12 + r, 4:36, :] = jnp.where(at_bottom, R.rim[1, r], R.pack[r * 32 : r * 32 + 32, :])
    for strip, above, below, left in ((3, 7, 5, 0), (2, 6, 4, 36)):
        R.pack[0:64, :] = R.fr[strip][...].astype(F32)
        R.pack[64:80, :] = R.fr[above][...].astype(F32)
        R.pack[80:96, :] = R.fr[below][...].astype(F32)
        for r in range(4):
            own = R.pack[r * 4 : r * 4 + 4, :]
            ext[r, left : left + 4, :] = jnp.where(at_top, own, R.pack[64 + r * 4 : 68 + r * 4, :])
            own = R.pack[48 + r * 4 : 52 + r * 4, :]
            ext[12 + r, left : left + 4, :] = jnp.where(at_bottom, own, R.pack[80 + r * 4 : 84 + r * 4, :])
        for r in range(8):
            ext[4 + r, left : left + 4, :] = R.pack[16 + r * 4 : 20 + r * 4, :]


def query_start(n):
    return n * 64 + (1 - n // 5) * 32


def forward_two(R):
    ext = R.ext
    for a in range(2):
        for b in range(5):
            for i in range(8):
                t = ((a * 5 + b) * 8 + i) * 8
                piece = ext[a * 8 + i, b * 8 : b * 8 + 8, :]
                R.x2[t : t + 8, :] = piece[:, 0:C]
                R.id2[t : t + 8, :] = jnp.broadcast_to(piece[:, C : C + 1], (8, 128))
    @pl.loop(0, 5)
    def _(i):
        at = pl.ds(pl.multiple_of(i * 128, 128), 128)
        normed = stats(R.x2[at, :])[0].astype(BF16)
        R.n2[at, :] = normed
        for ref, weight in ((R.k2, R.wk), (R.v2, R.wv)):
            ref[at, :] = dot(normed, weight[1]).astype(BF16)

    for n in range(10):
        start = query_start(n)
        R.nq2[n * 32 : n * 32 + 32, :] = R.n2[start : start + 32, :]
        R.xq2[n * 32 : n * 32 + 32, :] = R.x2[start : start + 32, :]
    R.q2[...] = dot(R.nq2[...], R.wq[1]).astype(BF16)

    @pl.loop(0, 5)
    def _(b):
        done = []
        for n, first in ((b, 32), (b + 5, 0)):
            keys = pl.ds(pl.multiple_of(n * 64, 64), 64)
            queries = pl.ds(pl.multiple_of(n * 32, 32), 32)
            within = pl.ds(pl.multiple_of(n * 64 + first, 32), 32)
            z_heads = tile_ids(R.id2[keys, :])[1]
            z = tile_ids(R.id2[within, :])[0]
            bias = R.bias[1, first : first + 32, :]
            probs = softmax_window(R.q2[queries, :], by_heads(R.k2[keys, :]), z, z_heads, bias)
            mix = dot(probs.astype(BF16), by_heads(R.v2[keys, :])).astype(BF16)
            done.append((queries, probs, mix))
        for queries, probs, mix in done:
            R.p2[queries, :] = probs
            R.mix2[queries, :] = mix

    @pl.loop(0, 2)
    def _(i):
        at = pl.ds(pl.multiple_of(i * 160, 32), 160)
        middle = (R.xq2[at, :] + dot(R.mix2[at, :], R.proj_w[1])).astype(BF16).astype(F32)
        normed = stats(middle)[0].astype(BF16)
        R.m2[at, :] = normed
        act, slope = gelu_parts(dot(normed, R.inner_w[1]))
        R.act2[at, :] = act.astype(BF16)
        grad_out = R.g2[at, :]
        grad_pre = (slope * dot(grad_out.astype(BF16), R.outer_w[1])).astype(BF16)
        R.pre2[at, :] = grad_pre
        grad_mid = (grad_out + norm_back(middle, dot_t(grad_pre, R.inner_w[1]))).astype(BF16)
        R.gm2[at, :] = grad_mid
        R.e2[at, :] = dot_t(grad_mid, R.proj_w[1]).astype(BF16)


def window_back(probs, e, q, k_heads, v_heads):
    grad_probs = dot_t(e, v_heads)
    grad_scores = probs * (grad_probs - head_reduce(grad_probs * probs, jnp.sum, 0.0))
    low = grad_scores.astype(BF16)
    grad_q = (dot(low, k_heads) * SCALE).astype(BF16)
    grad_k = (gather_heads(t_dot(low, q)) * SCALE).astype(BF16)
    grad_v = gather_heads(t_dot(probs.astype(BF16), e)).astype(BF16)
    return grad_scores, grad_q, grad_k, grad_v


def attend_back_two(R):
    R.gb[1] = jnp.zeros((64, 384), F32)

    @pl.loop(0, 5)
    def _(b):
        done = []
        for n in (b, b + 5):
            keys = pl.ds(pl.multiple_of(n * 64, 64), 64)
            queries = pl.ds(pl.multiple_of(n * 32, 32), 32)
            back = window_back(
                R.p2[queries, :],
                R.e2[queries, :],
                R.q2[queries, :],
                by_heads(R.k2[keys, :]),
                by_heads(R.v2[keys, :]),
            )
            done.append((keys, queries, back))
        for half, (keys, queries, back) in zip((32, 0), done):
            R.gb[1, half : half + 32, :] = R.gb[1, half : half + 32, :] + back[0]
            R.dq2[queries, :] = back[1]
            R.dk2[keys, :] = back[2]
            R.dv2[keys, :] = back[3]

    R.dnq2[...] = dot_t(R.dq2[...], R.wq[1])

    @pl.loop(0, 5)
    def _(i):
        at = pl.ds(pl.multiple_of(i * 128, 128), 128)
        R.dn2[at, :] = dot_t(R.dk2[at, :], R.wk[1]) + dot_t(R.dv2[at, :], R.wv[1])

    @pl.loop(0, 10)
    def _(n):
        queries = pl.ds(pl.multiple_of(n * 32, 32), 32)
        within = pl.ds(pl.multiple_of(query_start(n), 32), 32)
        R.dn2[within, :] = R.dn2[within, :] + R.dnq2[queries, :]

    @pl.loop(0, 5)
    def _(i):
        at = pl.ds(pl.multiple_of(i * 128, 128), 128)
        R.dn2[at, :] = norm_back(R.x2[at, :], R.dn2[at, :])

    @pl.loop(0, 10)
    def _(n):
        queries = pl.ds(pl.multiple_of(n * 32, 32), 32)
        within = pl.ds(pl.multiple_of(query_start(n), 32), 32)
        R.dn2[within, :] = R.dn2[within, :] + R.gm2[queries, :].astype(F32)


def back_copy(R, N, side):
    dr, dc = SIDES[side]
    return remote(R.bs[side], R.br[side], R.bsend.at[side], R.brecv.at[side], N.near(dr, dc))


def send_back(R, N):
    ext = R.dext
    for a in range(2):
        for b in range(5):
            for i in range(8):
                t = ((a * 5 + b) * 8 + i) * 8
                ext[a * 8 + i, b * 8 : b * 8 + 8, :] = R.dn2[t : t + 8, :]
    pack = R.pack
    for side, top in ((0, 0), (1, 12)):
        for r in range(4):
            pack[r * 32 : r * 32 + 32, 0:C] = ext[top + r, 4:36, :]
        R.bs[side][...] = pack[0:128, 0:C].astype(BF16)
    for side, left in ((2, 0), (3, 36)):
        for r in range(8):
            pack[r * 4 : r * 4 + 4, 0:C] = ext[4 + r, left : left + 4, :]
        R.bs[side][...] = pack[0:32, 0:C].astype(BF16)
    for side, top, left in ((4, 0, 0), (5, 0, 36), (6, 12, 0), (7, 12, 36)):
        for r in range(4):
            pack[r * 4 : r * 4 + 4, 0:C] = ext[top + r, left : left + 4, :]
        R.bs[side][...] = pack[0:16, 0:C].astype(BF16)
    for side in range(8):
        back_copy(R, N, side).start()


def receive_back(R, N):
    for side in range(8):
        back_copy(R, N, side).wait()
    ext, pack = R.dext, R.pack
    above = jnp.where(N.r == 0, 0.0, 1.0).astype(F32)
    below = jnp.where(N.r == 15, 0.0, 1.0).astype(F32)
    pack[...] = jnp.zeros_like(pack)
    for side, top, left, rows, cols, keep in (
        (1, 4, 4, 4, 32, above),
        (0, 8, 4, 4, 32, below),
        (3, 4, 4, 8, 4, None),
        (2, 4, 32, 8, 4, None),
        (7, 4, 4, 4, 4, above),
        (6, 4, 32, 4, 4, above),
        (5, 8, 4, 4, 4, below),
        (4, 8, 32, 4, 4, below),
    ):
        received = R.br[side][...].astype(F32)
        if keep is not None:
            received = jnp.where(keep > 0.5, received, 0.0)
        pack[0 : BACK_ROWS[side], 0:C] = received
        for r in range(rows):
            ext[top + r, left : left + cols, :] = (
                ext[top + r, left : left + cols, :] + pack[r * cols : r * cols + cols, 0:C]
            )
    for w in range(4):
        for r in range(8):
            t = w * 64 + r * 8
            R.g1[t : t + 8, :] = ext[4 + r, 4 + w * 8 : 12 + w * 8, :]


def channel_back_one(R):
    @pl.loop(0, 2)
    def _(i):
        at = pl.ds(pl.multiple_of(i * 128, 128), 128)
        grad_out = R.g1[at, :].astype(BF16)
        R.gf1[at, :] = grad_out
        grad_pre = (R.slope1[at, :] * dot(grad_out, R.outer_w[0])).astype(BF16)
        R.pre1[at, :] = grad_pre
        back = norm_back(R.mid1[at, :], dot_t(grad_pre, R.inner_w[0]))
        grad_mid = (grad_out.astype(F32) + back).astype(BF16)
        R.gm1[at, :] = grad_mid
        R.e1[at, :] = dot_t(grad_mid, R.proj_w[0]).astype(BF16)


def attend_back_one(R):
    R.gb[0] = jnp.zeros((64, 384), F32)

    @pl.loop(0, 2)
    def _(pair):
        done = []
        for w in (pair * 2, pair * 2 + 1):
            at = pl.ds(pl.multiple_of(w * 64, 64), 64)
            back = window_back(
                R.p1[at, :], R.e1[at, :], R.q1[at, :], by_heads(R.k1[at, :]), by_heads(R.v1[at, :])
            )
            done.append((at, back))
        for at, back in done:
            R.gb[0] = R.gb[0] + back[0]
            R.dq1[at, :] = back[1]
            R.dk1[at, :] = back[2]
            R.dv1[at, :] = back[3]


def finish_one(R):
    @pl.loop(0, 2)
    def _(i):
        at = pl.ds(pl.multiple_of(i * 128, 128), 128)
        grad = dot_t(R.dq1[at, :], R.wq[0])
        grad = grad + dot_t(R.dk1[at, :], R.wk[0]) + dot_t(R.dv1[at, :], R.wv[0])
        R.x1[at, :] = R.gm1[at, :].astype(F32) + norm_back(R.x1[at, :], grad)

    for r in range(8):
        row = [R.x1[w * 64 + r * 8 : w * 64 + r * 8 + 8, :] for w in range(4)]
        R.token_grad[r] = jnp.concatenate(row, axis=0).astype(BF16)


def grads_of(R, b):
    pick = R.pick_ch[...]
    normed = dot((R.n1, R.n2)[b][...], pick).astype(BF16)
    query_normed = dot(R.nq2[...], pick).astype(BF16) if b else normed
    R.t_qkv[0:C, :] = t_dot((R.dq1, R.dq2)[b][...], query_normed)
    R.t_qkv[C : 2 * C, :] = t_dot((R.dk1, R.dk2)[b][...], normed)
    R.t_qkv[2 * C : 3 * C, :] = t_dot((R.dv1, R.dv2)[b][...], normed)
    R.t_proj[...] = t_dot((R.gm1, R.gm2)[b][...], dot((R.mix1, R.mix2)[b][...], pick).astype(BF16))
    R.t_inner[...] = t_dot((R.pre1, R.pre2)[b][...], dot((R.m1, R.m2)[b][...], pick).astype(BF16))
    grad_out = R.g2[...].astype(BF16) if b else R.gf1[...]
    for s in range(4):
        act = dot((R.act1, R.act2)[b][...], R.pick_hid[:, s * 256 : s * 256 + 256]).astype(BF16)
        R.t_outer[s] = t_dot(grad_out, act)

    @pl.loop(0, 8)
    def _(y):
        def part(ref, width):
            return ref[pl.ds(pl.multiple_of(y * width, 8), width), :]

        stacked = [part(R.t_qkv, 72), part(R.t_proj, 24), part(R.t_inner, 96)]
        stacked += [part(R.t_outer.at[s], 24) for s in range(4)]
        chunks = dot(R.cut[...], jnp.concatenate(stacked, axis=0).astype(BF16)).astype(BF16)
        for q in range(4):
            for x_lo in range(2):
                R.ga[b, q % 2, q // 2 * 2 + x_lo, y] = chunks[
                    q * CHUNK : q * CHUNK + CHUNK, x_lo * 128 : x_lo * 128 + 128
                ]


def table_of(R, b):
    R.tab[b * 8 : b * 8 + 8, :] = fold_bias(R.gb.at[b], R.offsets)


def core_copy(R, N, b):
    return remote(
        R.ga.at[b, 1 - N.core], R.ra.at[b], R.asend.at[b], R.arecv.at[b], N.partner()
    )


def start_core(R, N, b):
    core_copy(R, N, b).start()


def start_table(R, N):
    R.ta[...] = R.tab[...].astype(BF16)
    table_copy(R, N).start()


def table_copy(R, N):
    return remote(R.ta, R.rta, R.tsend.at[0], R.trecv.at[0], N.partner())


def spread_copies(R, send, recv, src, dst, base, me, n, device):
    def sending(other, d):
        return remote(src(other), dst(me), send.at[base + d], recv.at[base + me], device(other))

    def arriving(other, d):
        return remote(src(other), dst(other), send.at[base + d], recv.at[base + other], device(other))

    return [(functools.partial(sending, (me + d) % n, d), functools.partial(arriving, (me + d) % n, d)) for d in range(1, n)]


def x_copies(R, N, b):
    return spread_copies(
        R, R.xsend, R.xrecv, lambda o: R.hb.at[b, o], lambda s: R.rb.at[b, s], b * 4, N.x, 4, N.at_x
    )


def y_copies(R, N, b):
    return spread_copies(
        R, R.ysend, R.yrecv, lambda o: R.hc.at[b, o], lambda s: R.rc.at[b, s], b * 8, N.y, 8, N.at_y
    )


def z_copies(R, N, b):
    return spread_copies(
        R, R.zsend, R.zrecv, lambda o: R.hd.at[b, o], lambda s: R.rd.at[b, s], b * 8, N.z, 8, N.at_z
    )


def table_copies(R, N, stage):
    me, n, device = ((N.x, 4, N.at_x), (N.y, 8, N.at_y), (N.z, 8, N.at_z))[stage]
    base = stage * 8
    src, dst = R.table_out[stage], R.table_in[stage]
    return spread_copies(
        R, R.tbsend, R.tbrecv, lambda o: src, lambda s: dst.at[s], base, me, n, device
    )


def go(copies):
    for sending, _ in copies:
        sending().start()


def settle(copies):
    for sending, arriving in copies:
        sending().wait_send()
        arriving().wait_recv()


def table_sum(R, N, stage):
    settle(table_copies(R, N, stage))
    n = 8 if stage else 4
    received = R.table_in[stage]
    total = received[0].astype(F32)
    for s in range(1, n):
        total = total + received[s].astype(F32)
    return total


def table_send(R, N, stage, total):
    me = (N.x, N.y, N.z)[stage]
    low = total.astype(BF16)
    R.table_out[stage][...] = low
    R.table_in[stage][me] = low
    go(table_copies(R, N, stage))


def start_x(R, N, b):
    core_copy(R, N, b).wait()

    @pl.loop(0, 4)
    def _(x):
        for y in range(8):
            total = R.ga[b, N.core, x, y].astype(F32) + R.ra[b, x, y].astype(F32)
            R.hb[b, x, y] = total.astype(BF16)

    go(x_copies(R, N, b))
    if b == 0:
        table_copy(R, N).wait()
        table_send(R, N, 0, R.ta[...].astype(F32) + R.rta[...].astype(F32))


def start_y(R, N, b):
    settle(x_copies(R, N, b))

    @pl.loop(0, 8)
    def _(y):
        total = R.hb[b, N.x, y].astype(F32)
        for d in range(1, 4):
            total = total + R.rb[b, (N.x + d) % 4, y].astype(F32)
        R.hc[b, y] = total.astype(BF16)

    go(y_copies(R, N, b))
    if b == 0:
        table_send(R, N, 1, table_sum(R, N, 0))


def start_z(R, N, b):
    settle(y_copies(R, N, b))
    total = R.hc[b, N.y].astype(F32)
    for d in range(1, 8):
        total = total + R.rc[b, (N.y + d) % 8].astype(F32)
    R.turn[...] = jnp.concatenate([total, jnp.zeros((128 - CHUNK, 128), F32)], axis=0).T
    for z in range(8):
        R.hd[b, z] = R.turn[z * 12 : z * 12 + 16, :].astype(BF16)
    go(z_copies(R, N, b))
    if b == 0:
        table_send(R, N, 2, table_sum(R, N, 1))


def finish_z(R, N, b):
    settle(z_copies(R, N, b))
    total = R.hd[b, N.z].astype(F32)
    for d in range(1, 8):
        total = total + R.rd[b, (N.z + d) % 8].astype(F32)
    R.totals[b] = total
    if b == 0:
        R.table_total[...] = table_sum(R, N, 2)


def hand_on(summed, totals, table, tokens, qkv, proj, inner, outer, table_grad):
    tokens[...] = summed[...]
    for b in range(2):
        total = totals[b] * (1.0 / 512.0)
        qkv[:, b, :] = total[0:12, 0:18]
        inner[:, b, :] = total[0:12, 24:48]
        turned = jnp.concatenate([total, jnp.zeros((112, 128), F32)], axis=0).T
        proj[:, b, :] = turned[18:24, 0:12]
        parts = [turned[48 + 6 * s : 54 + 6 * s, 0:12] for s in range(4)]
        outer[:, b, :] = jnp.concatenate(parts, axis=1)
        table_grad[:, b, :] = table[b * 8 : b * 8 + 6, 0:225] * (1.0 / 512.0)


def scratch():
    def f(*shape):
        return pltpu.VMEM(shape, F32)

    def h(*shape):
        return pltpu.VMEM(shape, BF16)

    def semaphores(count):
        return pltpu.SemaphoreType.DMA((count,))

    out = dict(wq=h(2, C, C), wk=h(2, C, C), wv=h(2, C, C), bias=f(2, 64, 384))
    out.update(x1=f(256, C), id1=f(256, 128), rim_id=f(2, 128, 128), rim=f(2, 4, 32, CW))
    out.update(pick_hid=h(HID, 1024), pick_ch=h(C, 256), cut=h(4 * CHUNK, 288))
    out.update(n1=h(256, C), q1=h(256, C), k1=h(256, C), v1=h(256, C), mix1=h(256, C), m1=h(256, C))
    out.update(gf1=h(256, C), gm1=h(256, C), e1=h(256, C), dq1=h(256, C), dk1=h(256, C), dv1=h(256, C))
    out.update(p1=f(256, 384), mid1=f(256, C), first=f(256, C), g1=f(256, C))
    out.update(act1=h(256, HID), slope1=f(256, HID), pre1=h(256, HID))
    out.update(ext=f(16, 40, CW), dext=f(16, 40, C), cot_ext=f(8, 40, C), pack=f(128, CW))
    out.update(x2=f(640, C), id2=f(640, 128), dn2=f(640, C))
    out.update(n2=h(640, C), k2=h(640, C), v2=h(640, C), dk2=h(640, C), dv2=h(640, C))
    out.update(nq2=h(320, C), q2=h(320, C), mix2=h(320, C), m2=h(320, C), gm2=h(320, C), e2=h(320, C), dq2=h(320, C))
    out.update(xq2=f(320, C), g2=f(320, C), dnq2=f(320, C), p2=f(320, 384))
    out.update(act2=h(320, HID), pre2=h(320, HID), gb=f(2, 64, 384))
    out.update(t_qkv=f(576, 256), t_proj=f(C, 256), t_inner=f(HID, 256), t_outer=f(4, C, 256))
    out.update(offsets=h(WIN, 256, 128), tab=f(16, 256), turn=f(128, 128))
    out.update(fs=[h(n, CW) for n in SIDE_ROWS], fr=[h(n, CW) for n in SIDE_ROWS])
    out.update(bs=[h(n, C) for n in BACK_ROWS], br=[h(n, C) for n in BACK_ROWS])
    out.update(ga=h(2, 2, 4, 8, CHUNK, 128), ra=h(2, 4, 8, CHUNK, 128))
    out.update(hb=h(2, 4, 8, CHUNK, 128), rb=h(2, 4, 8, CHUNK, 128))
    out.update(hc=h(2, 8, CHUNK, 128), rc=h(2, 8, CHUNK, 128), hd=h(2, 8, 16, 128), rd=h(2, 8, 16, 128))
    out.update(ta=h(16, 256), rta=h(16, 256), table_out=[h(16, 256)] * 3)
    out.update(table_in=[h(4, 16, 256), h(8, 16, 256), h(8, 16, 256)])
    out.update(fsend=semaphores(8), frecv=semaphores(8), bsend=semaphores(8), brecv=semaphores(8))
    out.update(asend=semaphores(2), arecv=semaphores(2), tsend=semaphores(1), trecv=semaphores(1))
    out.update(xsend=semaphores(8), xrecv=semaphores(8), ysend=semaphores(16), yrecv=semaphores(16))
    out.update(zsend=semaphores(16), zrecv=semaphores(16), tbsend=semaphores(24), tbrecv=semaphores(24))
    return out


SHAPES, STRUCTURE = jax.tree.flatten(scratch(), is_leaf=lambda x: not isinstance(x, (dict, list)))
COUNT = 15


def local(
    tokens,
    region_ids,
    upper_rim,
    upper_ids,
    lower_rim,
    lower_ids,
    cotangent,
    qkv_weight,
    proj_weight,
    inner_weight,
    outer_weight,
    bias_table,
):
    out = pl.pallas_call(
        body,
        out_shape=(
            jax.ShapeDtypeStruct((8, 32, C), BF16),
            jax.ShapeDtypeStruct((2, 16, 128), F32),
            jax.ShapeDtypeStruct((16, 256), F32),
        ),
        in_specs=[pl.BlockSpec(memory_space=pltpu.VMEM)] * 12,
        out_specs=[pl.BlockSpec(memory_space=pltpu.VMEM)] * 3,
        scratch_shapes=SHAPES,
        compiler_params=pltpu.CompilerParams(
            collective_id=0, has_side_effects=True, vmem_limit_bytes=60 * 1024 * 1024
        ),
        name="blocks",
    )(
        tokens,
        region_ids,
        upper_rim,
        upper_ids,
        lower_rim,
        lower_ids,
        cotangent,
        qkv_weight,
        proj_weight,
        inner_weight,
        outer_weight.transpose(0, 2, 1),
        bias_table.transpose(2, 0, 1),
    )
    out = pl.pallas_call(
        hand_on,
        out_shape=(
            jax.ShapeDtypeStruct((8, 32, C), BF16),
            jax.ShapeDtypeStruct((12, 2, 18), F32),
            jax.ShapeDtypeStruct((6, 2, 12), F32),
            jax.ShapeDtypeStruct((12, 2, 24), F32),
            jax.ShapeDtypeStruct((6, 2, 48), F32),
            jax.ShapeDtypeStruct((6, 2, 225), F32),
        ),
        in_specs=[pl.BlockSpec(memory_space=pltpu.VMEM)] * 3,
        out_specs=[pl.BlockSpec(memory_space=pltpu.VMEM)] * 6,
        name="hand_on",
    )(*out)
    orders = ((1, 0, 2), (1, 2, 0), (1, 0, 2), (1, 2, 0), (1, 2, 0))
    return (out[0], *(part.transpose(order) for part, order in zip(out[1:], orders)))


def solution(mesh):
    return jax.shard_map(
        local,
        mesh=mesh,
        in_specs=(
            P("rows", "cols", None),
            P("rows", "cols"),
            P(None, "cols", None),
            P(None, "cols"),
            P(None, "cols", None),
            P(None, "cols"),
            P("rows", "cols", None),
            P(),
            P(),
            P(),
            P(),
            P(),
        ),
        out_specs=(
            P("rows", "cols", None),
            P(None, "rows", "cols"),
            P(None, "rows", "cols"),
            P(None, "rows", "cols"),
            P(None, "rows", "cols"),
            P(),
        ),
        check_vma=False,
    )
```

```python
import functools
import math
import types

import jax
import jax.numpy as jnp
from jax import lax
from jax.experimental import pallas as pl
from jax.experimental.pallas import tpu as pltpu
from jax.sharding import PartitionSpec as P

C = 192
HEADS = 6
HD = 32
HID = 768
WIN = 8
HALF = 4
EPS = 1e-05
MASKED = -1000000000.0
SCALE = HD**-0.5
CW = 256
CHUNK = 80
TOP = 48
F32 = jnp.float32
BF16 = jnp.bfloat16
MESH = pl.DeviceIdType.MESH


def dot(a, b):
    return lax.dot_general(a, b, (((1,), (0,)), ((), ())), preferred_element_type=F32)


def dot_t(a, b):
    return lax.dot_general(a, b, (((1,), (1,)), ((), ())), preferred_element_type=F32)


def t_dot(a, b):
    return lax.dot_general(a, b, (((0,), (0,)), ((), ())), preferred_element_type=F32)


def iota(shape, dim):
    return lax.broadcasted_iota(jnp.int32, shape, dim)


def stats(values):
    center = jnp.sum(values, axis=-1, keepdims=True) * (1.0 / C)
    shifted = values - center
    spread = jnp.sum(shifted * shifted, axis=-1, keepdims=True) * (1.0 / C)
    inverse = lax.rsqrt(spread + EPS)
    return shifted * inverse, inverse


def norm_back(values, grad):
    hat, inverse = stats(values)
    mean_grad = jnp.sum(grad, axis=-1, keepdims=True) * (1.0 / C)
    mean_dot = jnp.sum(grad * hat, axis=-1, keepdims=True) * (1.0 / C)
    return inverse * (grad - mean_grad - hat * mean_dot)


def by_heads(values):
    lane_head = iota(values.shape, 1) // HD
    zero = jnp.zeros_like(values)
    return jnp.concatenate([jnp.where(lane_head == h, values, zero) for h in range(HEADS)], axis=0)


def gather_heads(stacked):
    lane_head = iota((64, C), 1) // HD
    total = jnp.zeros((64, C), F32)
    for h in range(HEADS):
        total = jnp.where(lane_head == h, stacked[h * 64 : h * 64 + 64], total)
    return total


def head_reduce(scores, reduce, fill):
    pieces = []
    for pair in range(3):
        part = scores[:, pair * 128 : pair * 128 + 128]
        first = iota(part.shape, 1) < 64
        low = reduce(jnp.where(first, part, fill), axis=-1, keepdims=True)
        high = reduce(jnp.where(first, fill, part), axis=-1, keepdims=True)
        pieces.append(jnp.where(first, low, high))
    return jnp.concatenate(pieces, axis=1)


def softmax_window(q, k_heads, z_q, z_heads, bias):
    scores = dot_t(q, k_heads) * SCALE + bias
    scores = jnp.where(dot_t(z_q, z_heads) > 0.5, scores, MASKED)
    exponent = jnp.exp(scores - head_reduce(scores, jnp.max, -jnp.inf))
    return exponent / head_reduce(exponent, jnp.sum, 0.0)


def tile_ids(ids):
    z = (iota(ids.shape, 1).astype(F32) == ids).astype(BF16)
    return z, jnp.concatenate([z] * HEADS, axis=0)


def gelu_parts(pre):
    cdf = 0.5 * (1.0 + lax.erf(pre * (1.0 / math.sqrt(2.0))))
    slope = cdf + pre * (jnp.exp(-0.5 * pre * pre) * (1.0 / math.sqrt(2.0 * math.pi)))
    return pre * cdf, slope


def split(values):
    high = values.astype(BF16)
    rest = values - high.astype(F32)
    middle = rest.astype(BF16)
    low = (rest - middle.astype(F32)).astype(BF16)
    return jnp.concatenate([high, middle, low], axis=0)


def joined(pieces):
    n = pieces.shape[0] // 3
    return pieces[0:n] + pieces[n : 2 * n] + pieces[2 * n :]


def offset_onehots(out_ref):
    lane = iota((1, 128), 1)
    row = iota((256, 128), 0)
    for ci in range(WIN):
        offset = jnp.where(lane < 120, (14 - lane // 8) * 15 + (ci - lane % 8 + 7), -1)
        out_ref[ci] = (row == offset).astype(BF16)


def spread_bias(R):
    R.tab[...] = jnp.zeros((16, 256), F32)
    for b in range(2):
        R.tab[b * 8 : b * 8 + 6, 0:225] = R.table[:, b, :]
    pieces = split(R.tab[...])
    per_column = [joined(dot(pieces, R.offsets[ci])) for ci in range(WIN)]
    first = iota((8, 128), 1) < 64
    for b in range(2):
        per_head = [
            jnp.concatenate([per_column[ci][b * 8 + h : b * 8 + h + 1] for ci in range(WIN)], axis=0)
            for h in range(HEADS)
        ]
        for ri in range(WIN):
            shift = (7 - ri) * 8
            for pair in range(3):
                low = pltpu.roll(per_head[2 * pair], (128 - shift) % 128, 1)
                high = pltpu.roll(per_head[2 * pair + 1], (64 - shift) % 128, 1)
                R.bias[b, ri * 8 : ri * 8 + 8, pair * 128 : pair * 128 + 128] = jnp.where(first, low, high)


def fold_bias(grad_ref, offsets):
    first = iota((8, 128), 1) < 64
    per_head = [jnp.zeros((8, 128), F32) for _ in range(HEADS)]
    for ri in range(WIN):
        shift = (7 - ri) * 8
        for pair in range(3):
            part = grad_ref[ri * 8 : ri * 8 + 8, pair * 128 : pair * 128 + 128]
            low = pltpu.roll(jnp.where(first, part, 0.0), shift % 128, 1)
            high = pltpu.roll(jnp.where(first, 0.0, part), (shift + 64) % 128, 1)
            per_head[2 * pair] = per_head[2 * pair] + low
            per_head[2 * pair + 1] = per_head[2 * pair + 1] + high
    total = jnp.zeros((8, 256), F32)
    for ci in range(WIN):
        rows = jnp.concatenate([per_head[h][ci : ci + 1] for h in range(HEADS)] + [jnp.zeros((2, 128), F32)], axis=0)
        total = total + joined(dot_t(split(rows), offsets[ci]))
    return total


def place():
    r = lax.axis_index("rows")
    c = lax.axis_index("cols")
    return r, c


class Net:
    def __init__(self):
        r, c = place()
        self.r, self.c = r, c
        self.x_lo, self.z = r // 8, r % 8
        self.y, self.x_hi, self.core = c // 4, (c // 2) % 2, c % 2
        self.x = self.x_hi * 2 + self.x_lo

    def near(self, dr, dc):
        return ((self.r + dr + 16) % 16, (self.c + dc + 32) % 32)

    def partner(self):
        return (self.r, self.c + 1 - 2 * self.core)

    def at_x(self, x):
        return ((x % 2) * 8 + self.z, self.y * 4 + (x // 2) * 2 + self.core)

    def at_y(self, y):
        return (self.r, y * 4 + self.x_hi * 2 + self.core)

    def at_z(self, z):
        return (self.x_lo * 8 + z, self.c)

    def everyone(self):
        peers = [self.near(dr, dc) for dr, dc in SIDES] + [self.partner()]
        peers += [self.at_x((self.x + d) % 4) for d in range(1, 4)]
        peers += [self.at_y((self.y + d) % 8) for d in range(1, 8)]
        peers += [self.at_z((self.z + d) % 8) for d in range(1, 8)]
        return peers


SIDES = ((-1, 0), (1, 0), (0, -1), (0, 1), (-1, -1), (-1, 1), (1, -1), (1, 1))
SIDE_ROWS = (128, 128, 64, 64, 16, 16, 16, 16)
BACK_ROWS = (128, 128, 32, 32, 16, 16, 16, 16)


def remote(src, dst, send, recv, device):
    return pltpu.make_async_remote_copy(
        src_ref=src, dst_ref=dst, send_sem=send, recv_sem=recv, device_id=device, device_id_type=MESH
    )


def body(*refs):
    R = types.SimpleNamespace(**jax.tree.unflatten(STRUCTURE, refs[COUNT:]))
    R.tokens, R.ids, R.upper, R.upper_ids, R.lower, R.lower_ids, R.cot = refs[:7]
    R.qkv_w, R.proj_w, R.inner_w, R.outer_w, R.table, R.token_grad, R.totals = refs[7:14]
    R.table_total = refs[14]
    N = Net()

    barrier = pltpu.get_barrier_semaphore()
    peers = N.everyone()
    for peer in peers:
        pl.semaphore_signal(barrier, inc=1, device_id=peer, device_id_type=MESH)

    setup(R)
    forward_one(R)
    pl.semaphore_wait(barrier, len(peers))
    exchange_forward(R, N)
    forward_two(R)
    attend_back_two(R)
    send_back(R, N)
    grads_of(R, 1)
    start_core(R, N, 1)
    table_of(R, 1)
    receive_back(R, N)
    channel_back_one(R)
    start_x(R, N, 1)
    attend_back_one(R)
    start_y(R, N, 1)
    grads_of(R, 0)
    start_core(R, N, 0)
    table_of(R, 0)
    start_table(R, N)
    finish_one(R)
    start_z(R, N, 1)
    start_x(R, N, 0)
    finish_z(R, N, 1)
    start_y(R, N, 0)
    start_z(R, N, 0)
    finish_z(R, N, 0)


def select_column(rows, order, ids):
    n = ids.shape[0]
    row_of, col_of = order
    pick = (iota((rows, n), 1) == row_of(iota((rows, n), 0))).astype(BF16)
    spread = dot(pick, ids.astype(F32).astype(BF16))
    keep = iota((rows, 32), 1) == col_of(iota((rows, 32), 0))
    column = jnp.sum(jnp.where(keep, spread, 0.0), axis=-1, keepdims=True)
    return jnp.broadcast_to(column, (rows, 128))


def setup(R):
    offset_onehots(R.offsets)
    spread_bias(R)
    for i, ref in enumerate((R.wq, R.wk, R.wv)):
        ref[0] = R.qkv_w[0][:, i * C : i * C + C]
    for r in range(8):
        row = R.tokens[r].astype(F32)
        for w in range(4):
            R.x1[w * 64 + r * 8 : w * 64 + r * 8 + 8, :] = row[w * 8 : w * 8 + 8]
    by_window = (lambda t: (t // 8) % 8, lambda t: (t // 64) * 8 + t % 8)
    by_row = (lambda t: t // 32, lambda t: t % 32)
    R.id1[...] = select_column(256, by_window, R.ids[...])
    R.rim_id[0] = select_column(128, by_row, R.upper_ids[...])
    R.rim_id[1] = select_column(128, by_row, R.lower_ids[...])


def setup_later(R):
    for i, ref in enumerate((R.wq, R.wk, R.wv)):
        ref[1] = R.qkv_w[1][:, i * C : i * C + C]
    R.cot_ext[...] = jnp.zeros_like(R.cot_ext)
    for r in range(8):
        R.cot_ext[r, 4:36, :] = R.cot[r].astype(F32)
    for a in range(2):
        for b in range(5):
            for i in range(4):
                t = (a * 5 + b) * 32 + i * 8
                R.g2[t : t + 8, :] = R.cot_ext[a * 4 + i, b * 8 : b * 8 + 8, :]
    lane = iota((1, 1024), 1)
    inside = lane % 128
    row = (lane // 128 % 2 * 8 + inside // 12) * 48 + lane // 256 * 12 + inside % 12
    row = jnp.where(inside < 96, row, -1)
    R.pick_hid[...] = (iota((HID, 1024), 0) == row).astype(BF16)
    lane = iota((1, 256), 1)
    inside = lane % 128
    row = jnp.where(inside < 96, lane // 128 * 96 + inside, -1)
    R.pick_ch[...] = (iota((C, 256), 0) == row).astype(BF16)
    out = iota((4 * CHUNK, 1), 0)
    q, k = out // CHUNK, out % CHUNK
    hid = (k - 48) // 6
    col = jnp.where(
        k < 18,
        18 * q + k,
        jnp.where(
            k < 24,
            72 + 6 * q + k - 18,
            jnp.where(k < 48, 96 + 24 * q + k - 24, 192 + 24 * hid + 6 * q + (k - 48 - 6 * hid)),
        ),
    )
    col = jnp.where(k < 72, col, -1)
    R.cut[...] = (iota((4 * CHUNK, 288), 1) == col).astype(BF16)


def forward_one(R):
    @pl.loop(0, 2)
    def _(i):
        at = pl.ds(pl.multiple_of(i * 128, 128), 128)
        normed = stats(R.x1[at, :])[0].astype(BF16)
        R.n1[at, :] = normed
        for ref, weight in ((R.q1, R.wq), (R.k1, R.wk), (R.v1, R.wv)):
            ref[at, :] = dot(normed, weight[0]).astype(BF16)

    @pl.loop(0, 2)
    def _(pair):
        done = []
        for w in (pair * 2, pair * 2 + 1):
            at = pl.ds(pl.multiple_of(w * 64, 64), 64)
            z, z_heads = tile_ids(R.id1[at, :])
            probs = softmax_window(R.q1[at, :], by_heads(R.k1[at, :]), z, z_heads, R.bias[0])
            mix = dot(probs.astype(BF16), by_heads(R.v1[at, :])).astype(BF16)
            done.append((at, probs, mix))
        for at, probs, mix in done:
            R.p1[at, :] = probs
            R.mix1[at, :] = mix

    @pl.loop(0, 2)
    def _(i):
        at = pl.ds(pl.multiple_of(i * 128, 128), 128)
        middle = (R.x1[at, :] + dot(R.mix1[at, :], R.proj_w[0])).astype(BF16).astype(F32)
        R.mid1[at, :] = middle
        normed = stats(middle)[0].astype(BF16)
        R.m1[at, :] = normed
        act, slope = gelu_parts(dot(normed, R.inner_w[0]))
        act = act.astype(BF16)
        R.act1[at, :] = act
        R.slope1[at, :] = slope
        R.first[at, :] = (middle + dot_t(act, R.outer_w[0])).astype(BF16).astype(F32)


def exchange_forward(R, N):
    ext = R.ext
    for w in range(4):
        for r in range(8):
            t = w * 64 + r * 8
            piece = jnp.concatenate([R.first[t : t + 8, :], R.id1[t : t + 8, 0:64]], axis=1)
            ext[4 + r, 4 + w * 8 : 12 + w * 8, :] = piece
    for i, rim in enumerate((R.upper, R.lower)):
        for r in range(4):
            row = rim[r].astype(F32)
            R.rim[i, r] = jnp.concatenate([row, R.rim_id[i, r * 32 : r * 32 + 32, 0:64]], axis=1)
    for side, top in ((0, 4), (1, 8)):
        for r in range(4):
            R.pack[r * 32 : r * 32 + 32, :] = ext[top + r, 4:36, :]
        R.fs[side][...] = R.pack[0:128, :].astype(BF16)
    for side, left in ((2, 4), (3, 32)):
        for r in range(4):
            R.pack[r * 4 : r * 4 + 4, :] = R.rim[0, r, left - 4 : left, :]
            R.pack[48 + r * 4 : 52 + r * 4, :] = R.rim[1, r, left - 4 : left, :]
        for r in range(8):
            R.pack[16 + r * 4 : 20 + r * 4, :] = ext[4 + r, left : left + 4, :]
        R.fs[side][...] = R.pack[0:64, :].astype(BF16)
    for side, top, left in ((4, 4, 4), (5, 4, 32), (6, 8, 4), (7, 8, 32)):
        for r in range(4):
            R.pack[r * 4 : r * 4 + 4, :] = ext[top + r, left : left + 4, :]
        R.fs[side][...] = R.pack[0:16, :].astype(BF16)
    copies = []
    for side, (dr, dc) in enumerate(SIDES):
        copies.append(
            remote(
                R.fs[side], R.fr[side], R.fsend.at[side], R.frecv.at[side], N.near(dr, dc)
            )
        )
        copies[-1].start()
    setup_later(R)
    for copy in copies:
        copy.wait()
    at_top = N.r == 0
    at_bottom = N.r == 15
    R.pack[...] = R.fr[1][...].astype(F32)
    for r in range(4):
        ext[r, 4:36, :] = jnp.where(at_top, R.rim[0, r], R.pack[r * 32 : r * 32 + 32, :])
    R.pack[...] = R.fr[0][...].astype(F32)
    for r in range(4):
        ext[12 + r, 4:36, :] = jnp.where(at_bottom, R.rim[1, r], R.pack[r * 32 : r * 32 + 32, :])
    for strip, above, below, left in ((3, 7, 5, 0), (2, 6, 4, 36)):
        R.pack[0:64, :] = R.fr[strip][...].astype(F32)
        R.pack[64:80, :] = R.fr[above][...].astype(F32)
        R.pack[80:96, :] = R.fr[below][...].astype(F32)
        for r in range(4):
            own = R.pack[r * 4 : r * 4 + 4, :]
            ext[r, left : left + 4, :] = jnp.where(at_top, own, R.pack[64 + r * 4 : 68 + r * 4, :])
            own = R.pack[48 + r * 4 : 52 + r * 4, :]
            ext[12 + r, left : left + 4, :] = jnp.where(at_bottom, own, R.pack[80 + r * 4 : 84 + r * 4, :])
        for r in range(8):
            ext[4 + r, left : left + 4, :] = R.pack[16 + r * 4 : 20 + r * 4, :]


def query_start(n):
    return n * 64 + (1 - n // 5) * 32


def forward_two(R):
    ext = R.ext
    for a in range(2):
        for b in range(5):
            for i in range(8):
                t = ((a * 5 + b) * 8 + i) * 8
                piece = ext[a * 8 + i, b * 8 : b * 8 + 8, :]
                R.x2[t : t + 8, :] = piece[:, 0:C]
                R.id2[t : t + 8, :] = jnp.broadcast_to(piece[:, C : C + 1], (8, 128))
    @pl.loop(0, 5)
    def _(i):
        at = pl.ds(pl.multiple_of(i * 128, 128), 128)
        normed = stats(R.x2[at, :])[0].astype(BF16)
        R.n2[at, :] = normed
        for ref, weight in ((R.k2, R.wk), (R.v2, R.wv)):
            ref[at, :] = dot(normed, weight[1]).astype(BF16)

    for n in range(10):
        start = query_start(n)
        R.nq2[n * 32 : n * 32 + 32, :] = R.n2[start : start + 32, :]
        R.xq2[n * 32 : n * 32 + 32, :] = R.x2[start : start + 32, :]
    R.q2[...] = dot(R.nq2[...], R.wq[1]).astype(BF16)

    @pl.loop(0, 5)
    def _(b):
        done = []
        for n, first in ((b, 32), (b + 5, 0)):
            keys = pl.ds(pl.multiple_of(n * 64, 64), 64)
            queries = pl.ds(pl.multiple_of(n * 32, 32), 32)
            within = pl.ds(pl.multiple_of(n * 64 + first, 32), 32)
            z_heads = tile_ids(R.id2[keys, :])[1]
            z = tile_ids(R.id2[within, :])[0]
            bias = R.bias[1, first : first + 32, :]
            probs = softmax_window(R.q2[queries, :], by_heads(R.k2[keys, :]), z, z_heads, bias)
            mix = dot(probs.astype(BF16), by_heads(R.v2[keys, :])).astype(BF16)
            done.append((queries, probs, mix))
        for queries, probs, mix in done:
            R.p2[queries, :] = probs
            R.mix2[queries, :] = mix

    @pl.loop(0, 2)
    def _(i):
        at = pl.ds(pl.multiple_of(i * 160, 32), 160)
        middle = (R.xq2[at, :] + dot(R.mix2[at, :], R.proj_w[1])).astype(BF16).astype(F32)
        normed = stats(middle)[0].astype(BF16)
        R.m2[at, :] = normed
        act, slope = gelu_parts(dot(normed, R.inner_w[1]))
        R.act2[at, :] = act.astype(BF16)
        grad_out = R.g2[at, :]
        grad_pre = (slope * dot(grad_out.astype(BF16), R.outer_w[1])).astype(BF16)
        R.pre2[at, :] = grad_pre
        grad_mid = (grad_out + norm_back(middle, dot_t(grad_pre, R.inner_w[1]))).astype(BF16)
        R.gm2[at, :] = grad_mid
        R.e2[at, :] = dot_t(grad_mid, R.proj_w[1]).astype(BF16)


def window_back(probs, e, q, k_heads, v_heads):
    grad_probs = dot_t(e, v_heads)
    grad_scores = probs * (grad_probs - head_reduce(grad_probs * probs, jnp.sum, 0.0))
    low = grad_scores.astype(BF16)
    grad_q = (dot(low, k_heads) * SCALE).astype(BF16)
    grad_k = (gather_heads(t_dot(low, q)) * SCALE).astype(BF16)
    grad_v = gather_heads(t_dot(probs.astype(BF16), e)).astype(BF16)
    return grad_scores, grad_q, grad_k, grad_v


def attend_back_two(R):
    R.gb[1] = jnp.zeros((64, 384), F32)

    @pl.loop(0, 5)
    def _(b):
        done = []
        for n in (b, b + 5):
            keys = pl.ds(pl.multiple_of(n * 64, 64), 64)
            queries = pl.ds(pl.multiple_of(n * 32, 32), 32)
            back = window_back(
                R.p2[queries, :],
                R.e2[queries, :],
                R.q2[queries, :],
                by_heads(R.k2[keys, :]),
                by_heads(R.v2[keys, :]),
            )
            done.append((keys, queries, back))
        for half, (keys, queries, back) in zip((32, 0), done):
            R.gb[1, half : half + 32, :] = R.gb[1, half : half + 32, :] + back[0]
            R.dq2[queries, :] = back[1]
            R.dk2[keys, :] = back[2]
            R.dv2[keys, :] = back[3]

    R.dnq2[...] = dot_t(R.dq2[...], R.wq[1])

    @pl.loop(0, 5)
    def _(i):
        at = pl.ds(pl.multiple_of(i * 128, 128), 128)
        R.dn2[at, :] = dot_t(R.dk2[at, :], R.wk[1]) + dot_t(R.dv2[at, :], R.wv[1])

    @pl.loop(0, 10)
    def _(n):
        queries = pl.ds(pl.multiple_of(n * 32, 32), 32)
        within = pl.ds(pl.multiple_of(query_start(n), 32), 32)
        R.dn2[within, :] = R.dn2[within, :] + R.dnq2[queries, :]

    @pl.loop(0, 5)
    def _(i):
        at = pl.ds(pl.multiple_of(i * 128, 128), 128)
        R.dn2[at, :] = norm_back(R.x2[at, :], R.dn2[at, :])

    @pl.loop(0, 10)
    def _(n):
        queries = pl.ds(pl.multiple_of(n * 32, 32), 32)
        within = pl.ds(pl.multiple_of(query_start(n), 32), 32)
        R.dn2[within, :] = R.dn2[within, :] + R.gm2[queries, :].astype(F32)


def back_copy(R, N, side):
    dr, dc = SIDES[side]
    return remote(R.bs[side], R.br[side], R.bsend.at[side], R.brecv.at[side], N.near(dr, dc))


def send_back(R, N):
    ext = R.dext
    for a in range(2):
        for b in range(5):
            for i in range(8):
                t = ((a * 5 + b) * 8 + i) * 8
                ext[a * 8 + i, b * 8 : b * 8 + 8, :] = R.dn2[t : t + 8, :]
    pack = R.pack
    for side, top in ((0, 0), (1, 12)):
        for r in range(4):
            pack[r * 32 : r * 32 + 32, 0:C] = ext[top + r, 4:36, :]
        R.bs[side][...] = pack[0:128, 0:C].astype(BF16)
    for side, left in ((2, 0), (3, 36)):
        for r in range(8):
            pack[r * 4 : r * 4 + 4, 0:C] = ext[4 + r, left : left + 4, :]
        R.bs[side][...] = pack[0:32, 0:C].astype(BF16)
    for side, top, left in ((4, 0, 0), (5, 0, 36), (6, 12, 0), (7, 12, 36)):
        for r in range(4):
            pack[r * 4 : r * 4 + 4, 0:C] = ext[top + r, left : left + 4, :]
        R.bs[side][...] = pack[0:16, 0:C].astype(BF16)
    for side in range(8):
        back_copy(R, N, side).start()


def receive_back(R, N):
    for side in range(8):
        back_copy(R, N, side).wait()
    ext, pack = R.dext, R.pack
    above = jnp.where(N.r == 0, 0.0, 1.0).astype(F32)
    below = jnp.where(N.r == 15, 0.0, 1.0).astype(F32)
    pack[...] = jnp.zeros_like(pack)
    for side, top, left, rows, cols, keep in (
        (1, 4, 4, 4, 32, above),
        (0, 8, 4, 4, 32, below),
        (3, 4, 4, 8, 4, None),
        (2, 4, 32, 8, 4, None),
        (7, 4, 4, 4, 4, above),
        (6, 4, 32, 4, 4, above),
        (5, 8, 4, 4, 4, below),
        (4, 8, 32, 4, 4, below),
    ):
        received = R.br[side][...].astype(F32)
        if keep is not None:
            received = jnp.where(keep > 0.5, received, 0.0)
        pack[0 : BACK_ROWS[side], 0:C] = received
        for r in range(rows):
            ext[top + r, left : left + cols, :] = (
                ext[top + r, left : left + cols, :] + pack[r * cols : r * cols + cols, 0:C]
            )
    for w in range(4):
        for r in range(8):
            t = w * 64 + r * 8
            R.g1[t : t + 8, :] = ext[4 + r, 4 + w * 8 : 12 + w * 8, :]


def channel_back_one(R):
    @pl.loop(0, 2)
    def _(i):
        at = pl.ds(pl.multiple_of(i * 128, 128), 128)
        grad_out = R.g1[at, :].astype(BF16)
        R.gf1[at, :] = grad_out
        grad_pre = (R.slope1[at, :] * dot(grad_out, R.outer_w[0])).astype(BF16)
        R.pre1[at, :] = grad_pre
        back = norm_back(R.mid1[at, :], dot_t(grad_pre, R.inner_w[0]))
        grad_mid = (grad_out.astype(F32) + back).astype(BF16)
        R.gm1[at, :] = grad_mid
        R.e1[at, :] = dot_t(grad_mid, R.proj_w[0]).astype(BF16)


def attend_back_one(R):
    R.gb[0] = jnp.zeros((64, 384), F32)

    @pl.loop(0, 2)
    def _(pair):
        done = []
        for w in (pair * 2, pair * 2 + 1):
            at = pl.ds(pl.multiple_of(w * 64, 64), 64)
            back = window_back(
                R.p1[at, :], R.e1[at, :], R.q1[at, :], by_heads(R.k1[at, :]), by_heads(R.v1[at, :])
            )
            done.append((at, back))
        for at, back in done:
            R.gb[0] = R.gb[0] + back[0]
            R.dq1[at, :] = back[1]
            R.dk1[at, :] = back[2]
            R.dv1[at, :] = back[3]


def finish_one(R):
    @pl.loop(0, 2)
    def _(i):
        at = pl.ds(pl.multiple_of(i * 128, 128), 128)
        grad = dot_t(R.dq1[at, :], R.wq[0])
        grad = grad + dot_t(R.dk1[at, :], R.wk[0]) + dot_t(R.dv1[at, :], R.wv[0])
        R.x1[at, :] = R.gm1[at, :].astype(F32) + norm_back(R.x1[at, :], grad)

    for r in range(8):
        row = [R.x1[w * 64 + r * 8 : w * 64 + r * 8 + 8, :] for w in range(4)]
        R.token_grad[r] = jnp.concatenate(row, axis=0).astype(BF16)


def grads_of(R, b):
    pick = R.pick_ch[...]
    normed = dot((R.n1, R.n2)[b][...], pick).astype(BF16)
    query_normed = dot(R.nq2[...], pick).astype(BF16) if b else normed
    R.t_qkv[0:C, :] = t_dot((R.dq1, R.dq2)[b][...], query_normed)
    R.t_qkv[C : 2 * C, :] = t_dot((R.dk1, R.dk2)[b][...], normed)
    R.t_qkv[2 * C : 3 * C, :] = t_dot((R.dv1, R.dv2)[b][...], normed)
    R.t_proj[...] = t_dot((R.gm1, R.gm2)[b][...], dot((R.mix1, R.mix2)[b][...], pick).astype(BF16))
    R.t_inner[...] = t_dot((R.pre1, R.pre2)[b][...], dot((R.m1, R.m2)[b][...], pick).astype(BF16))
    grad_out = R.g2[...].astype(BF16) if b else R.gf1[...]
    for s in range(4):
        act = dot((R.act1, R.act2)[b][...], R.pick_hid[:, s * 256 : s * 256 + 256]).astype(BF16)
        R.t_outer[s] = t_dot(grad_out, act)

    @pl.loop(0, 8)
    def _(y):
        def part(ref, width):
            return ref[pl.ds(pl.multiple_of(y * width, 8), width), :]

        stacked = [part(R.t_qkv, 72), part(R.t_proj, 24), part(R.t_inner, 96)]
        stacked += [part(R.t_outer.at[s], 24) for s in range(4)]
        chunks = dot(R.cut[...], jnp.concatenate(stacked, axis=0).astype(BF16)).astype(BF16)
        for q in range(4):
            for x_lo in range(2):
                R.ga[b, q % 2, q // 2 * 2 + x_lo, y] = chunks[
                    q * CHUNK : q * CHUNK + CHUNK, x_lo * 128 : x_lo * 128 + 128
                ]


def table_of(R, b):
    R.tab[b * 8 : b * 8 + 8, :] = fold_bias(R.gb.at[b], R.offsets)


def core_copy(R, N, b):
    return remote(
        R.ga.at[b, 1 - N.core], R.ra.at[b], R.asend.at[b], R.arecv.at[b], N.partner()
    )


def start_core(R, N, b):
    core_copy(R, N, b).start()


def start_table(R, N):
    R.ta[...] = R.tab[...].astype(BF16)
    table_copy(R, N).start()


def table_copy(R, N):
    return remote(R.ta, R.rta, R.tsend.at[0], R.trecv.at[0], N.partner())


def spread_copies(R, send, recv, src, dst, base, me, n, device):
    def sending(other, d):
        return remote(src(other), dst(me), send.at[base + d], recv.at[base + me], device(other))

    def arriving(other, d):
        return remote(src(other), dst(other), send.at[base + d], recv.at[base + other], device(other))

    return [(functools.partial(sending, (me + d) % n, d), functools.partial(arriving, (me + d) % n, d)) for d in range(1, n)]


def x_copies(R, N, b):
    def source(other):
        return R.hb.at[b, other, :, 0:TOP, :]

    return spread_copies(R, R.xsend, R.xrecv, source, lambda s: R.rb.at[b, s], b * 4, N.x, 4, N.at_x)


def y_copies(R, N, b):
    return spread_copies(
        R, R.ysend, R.yrecv, lambda o: R.hc.at[b, o], lambda s: R.rc.at[b, s], b * 8, N.y, 8, N.at_y
    )


def y_first_copies(R, N, b):
    def source(other):
        return R.hb.at[b, :, other, TOP:CHUNK, :]

    return spread_copies(R, R.vsend, R.vrecv, source, lambda s: R.rv.at[b, s], b * 8, N.y, 8, N.at_y)


def x_second_copies(R, N, b):
    return spread_copies(
        R, R.wsend, R.wrecv, lambda o: R.hw.at[b, o], lambda s: R.rw.at[b, s], b * 4, N.x, 4, N.at_x
    )


def z_copies(R, N, b):
    return spread_copies(
        R, R.zsend, R.zrecv, lambda o: R.hd.at[b, o], lambda s: R.rd.at[b, s], b * 8, N.z, 8, N.at_z
    )


def table_copies(R, N, stage):
    me, n, device = ((N.x, 4, N.at_x), (N.y, 8, N.at_y), (N.z, 8, N.at_z))[stage]
    base = stage * 8
    src, dst = R.table_out[stage], R.table_in[stage]
    return spread_copies(
        R, R.tbsend, R.tbrecv, lambda o: src, lambda s: dst.at[s], base, me, n, device
    )


def go(copies):
    for sending, _ in copies:
        sending().start()


def settle(copies):
    for sending, arriving in copies:
        sending().wait_send()
        arriving().wait_recv()


def table_sum(R, N, stage):
    settle(table_copies(R, N, stage))
    n = 8 if stage else 4
    received = R.table_in[stage]
    total = received[0].astype(F32)
    for s in range(1, n):
        total = total + received[s].astype(F32)
    return total


def table_send(R, N, stage, total):
    me = (N.x, N.y, N.z)[stage]
    low = total.astype(BF16)
    R.table_out[stage][...] = low
    R.table_in[stage][me] = low
    go(table_copies(R, N, stage))


def start_x(R, N, b):
    core_copy(R, N, b).wait()

    over_x = x_copies(R, N, b)
    for d in (1, 3, 2, 0):
        x = (N.x + d) % 4
        for y in range(8):
            total = R.ga[b, N.core, x, y].astype(F32) + R.ra[b, x, y].astype(F32)
            R.hb[b, x, y] = total.astype(BF16)
        if d:
            go(over_x[d - 1 : d])
    go(y_first_copies(R, N, b))
    if b == 0:
        table_copy(R, N).wait()
        table_send(R, N, 0, R.ta[...].astype(F32) + R.rta[...].astype(F32))


def start_y(R, N, b):
    settle(x_copies(R, N, b))

    @pl.loop(0, 8)
    def _(y):
        total = R.hb[b, N.x, y, 0:TOP, :].astype(F32)
        for d in range(1, 4):
            total = total + R.rb[b, (N.x + d) % 4, y].astype(F32)
        R.hc[b, y] = total.astype(BF16)

    go(y_copies(R, N, b))
    settle(y_first_copies(R, N, b))
    for x in range(4):
        total = R.hb[b, x, N.y, TOP:CHUNK, :].astype(F32)
        for d in range(1, 8):
            total = total + R.rv[b, (N.y + d) % 8, x].astype(F32)
        R.hw[b, x] = total.astype(BF16)
    go(x_second_copies(R, N, b))
    if b == 0:
        table_send(R, N, 1, table_sum(R, N, 0))


def start_z(R, N, b):
    settle(y_copies(R, N, b))
    total = R.hc[b, N.y].astype(F32)
    for d in range(1, 8):
        total = total + R.rc[b, (N.y + d) % 8].astype(F32)
    settle(x_second_copies(R, N, b))
    rest = R.hw[b, N.x].astype(F32)
    for d in range(1, 4):
        rest = rest + R.rw[b, (N.x + d) % 4].astype(F32)
    R.turn[...] = jnp.concatenate([total, rest, jnp.zeros((128 - CHUNK, 128), F32)], axis=0).T
    for z in range(8):
        R.hd[b, z] = R.turn[z * 12 : z * 12 + 16, :].astype(BF16)
    go(z_copies(R, N, b))
    if b == 0:
        table_send(R, N, 2, table_sum(R, N, 1))


def finish_z(R, N, b):
    settle(z_copies(R, N, b))
    total = R.hd[b, N.z].astype(F32)
    for d in range(1, 8):
        total = total + R.rd[b, (N.z + d) % 8].astype(F32)
    R.totals[b] = total
    if b == 0:
        R.table_total[...] = table_sum(R, N, 2)


def hand_on(summed, totals, table, tokens, qkv, proj, inner, outer, table_grad):
    tokens[...] = summed[...]
    for b in range(2):
        total = totals[b] * (1.0 / 512.0)
        qkv[:, b, :] = total[0:12, 0:18]
        inner[:, b, :] = total[0:12, 24:48]
        turned = jnp.concatenate([total, jnp.zeros((112, 128), F32)], axis=0).T
        proj[:, b, :] = turned[18:24, 0:12]
        parts = [turned[48 + 6 * s : 54 + 6 * s, 0:12] for s in range(4)]
        outer[:, b, :] = jnp.concatenate(parts, axis=1)
        table_grad[:, b, :] = table[b * 8 : b * 8 + 6, 0:225] * (1.0 / 512.0)


def scratch():
    def f(*shape):
        return pltpu.VMEM(shape, F32)

    def h(*shape):
        return pltpu.VMEM(shape, BF16)

    def semaphores(count):
        return pltpu.SemaphoreType.DMA((count,))

    out = dict(wq=h(2, C, C), wk=h(2, C, C), wv=h(2, C, C), bias=f(2, 64, 384))
    out.update(x1=f(256, C), id1=f(256, 128), rim_id=f(2, 128, 128), rim=f(2, 4, 32, CW))
    out.update(pick_hid=h(HID, 1024), pick_ch=h(C, 256), cut=h(4 * CHUNK, 288))
    out.update(n1=h(256, C), q1=h(256, C), k1=h(256, C), v1=h(256, C), mix1=h(256, C), m1=h(256, C))
    out.update(gf1=h(256, C), gm1=h(256, C), e1=h(256, C), dq1=h(256, C), dk1=h(256, C), dv1=h(256, C))
    out.update(p1=f(256, 384), mid1=f(256, C), first=f(256, C), g1=f(256, C))
    out.update(act1=h(256, HID), slope1=f(256, HID), pre1=h(256, HID))
    out.update(ext=f(16, 40, CW), dext=f(16, 40, C), cot_ext=f(8, 40, C), pack=f(128, CW))
    out.update(x2=f(640, C), id2=f(640, 128), dn2=f(640, C))
    out.update(n2=h(640, C), k2=h(640, C), v2=h(640, C), dk2=h(640, C), dv2=h(640, C))
    out.update(nq2=h(320, C), q2=h(320, C), mix2=h(320, C), m2=h(320, C), gm2=h(320, C), e2=h(320, C), dq2=h(320, C))
    out.update(xq2=f(320, C), g2=f(320, C), dnq2=f(320, C), p2=f(320, 384))
    out.update(act2=h(320, HID), pre2=h(320, HID), gb=f(2, 64, 384))
    out.update(t_qkv=f(576, 256), t_proj=f(C, 256), t_inner=f(HID, 256), t_outer=f(4, C, 256))
    out.update(offsets=h(WIN, 256, 128), tab=f(16, 256), turn=f(128, 128))
    out.update(fs=[h(n, CW) for n in SIDE_ROWS], fr=[h(n, CW) for n in SIDE_ROWS])
    out.update(bs=[h(n, C) for n in BACK_ROWS], br=[h(n, C) for n in BACK_ROWS])
    out.update(ga=h(2, 2, 4, 8, CHUNK, 128), ra=h(2, 4, 8, CHUNK, 128))
    out.update(hb=h(2, 4, 8, CHUNK, 128), rb=h(2, 4, 8, TOP, 128))
    out.update(rv=h(2, 8, 4, CHUNK - TOP, 128), hw=h(2, 4, CHUNK - TOP, 128), rw=h(2, 4, CHUNK - TOP, 128))
    out.update(hc=h(2, 8, TOP, 128), rc=h(2, 8, TOP, 128), hd=h(2, 8, 16, 128), rd=h(2, 8, 16, 128))
    out.update(ta=h(16, 256), rta=h(16, 256), table_out=[h(16, 256)] * 3)
    out.update(table_in=[h(4, 16, 256), h(8, 16, 256), h(8, 16, 256)])
    out.update(fsend=semaphores(8), frecv=semaphores(8), bsend=semaphores(8), brecv=semaphores(8))
    out.update(asend=semaphores(2), arecv=semaphores(2), tsend=semaphores(1), trecv=semaphores(1))
    out.update(xsend=semaphores(8), xrecv=semaphores(8), ysend=semaphores(16), yrecv=semaphores(16))
    out.update(zsend=semaphores(16), zrecv=semaphores(16), tbsend=semaphores(24), tbrecv=semaphores(24))
    out.update(vsend=semaphores(16), vrecv=semaphores(16), wsend=semaphores(8), wrecv=semaphores(8))
    return out


SHAPES, STRUCTURE = jax.tree.flatten(scratch(), is_leaf=lambda x: not isinstance(x, (dict, list)))
COUNT = 15


def local(
    tokens,
    region_ids,
    upper_rim,
    upper_ids,
    lower_rim,
    lower_ids,
    cotangent,
    qkv_weight,
    proj_weight,
    inner_weight,
    outer_weight,
    bias_table,
):
    out = pl.pallas_call(
        body,
        out_shape=(
            jax.ShapeDtypeStruct((8, 32, C), BF16),
            jax.ShapeDtypeStruct((2, 16, 128), F32),
            jax.ShapeDtypeStruct((16, 256), F32),
        ),
        in_specs=[pl.BlockSpec(memory_space=pltpu.VMEM)] * 12,
        out_specs=[pl.BlockSpec(memory_space=pltpu.VMEM)] * 3,
        scratch_shapes=SHAPES,
        compiler_params=pltpu.CompilerParams(
            collective_id=0, has_side_effects=True, vmem_limit_bytes=60 * 1024 * 1024
        ),
        name="blocks",
    )(
        tokens,
        region_ids,
        upper_rim,
        upper_ids,
        lower_rim,
        lower_ids,
        cotangent,
        qkv_weight,
        proj_weight,
        inner_weight,
        outer_weight.transpose(0, 2, 1),
        bias_table.transpose(2, 0, 1),
    )
    out = pl.pallas_call(
        hand_on,
        out_shape=(
            jax.ShapeDtypeStruct((8, 32, C), BF16),
            jax.ShapeDtypeStruct((12, 2, 18), F32),
            jax.ShapeDtypeStruct((6, 2, 12), F32),
            jax.ShapeDtypeStruct((12, 2, 24), F32),
            jax.ShapeDtypeStruct((6, 2, 48), F32),
            jax.ShapeDtypeStruct((6, 2, 225), F32),
        ),
        in_specs=[pl.BlockSpec(memory_space=pltpu.VMEM)] * 3,
        out_specs=[pl.BlockSpec(memory_space=pltpu.VMEM)] * 6,
        name="hand_on",
    )(*out)
    orders = ((1, 0, 2), (1, 2, 0), (1, 0, 2), (1, 2, 0), (1, 2, 0))
    return (out[0], *(part.transpose(order) for part, order in zip(out[1:], orders)))


def solution(mesh):
    return jax.shard_map(
        local,
        mesh=mesh,
        in_specs=(
            P("rows", "cols", None),
            P("rows", "cols"),
            P(None, "cols", None),
            P(None, "cols"),
            P(None, "cols", None),
            P(None, "cols"),
            P("rows", "cols", None),
            P(),
            P(),
            P(),
            P(),
            P(),
        ),
        out_specs=(
            P("rows", "cols", None),
            P(None, "rows", "cols"),
            P(None, "rows", "cols"),
            P(None, "rows", "cols"),
            P(None, "rows", "cols"),
            P(),
        ),
        check_vma=False,
    )
```

```python
import functools
import math
import types

import jax
import jax.numpy as jnp
from jax import lax
from jax.experimental import pallas as pl
from jax.experimental.pallas import tpu as pltpu
from jax.sharding import PartitionSpec as P

C = 192
HEADS = 6
HD = 32
HID = 768
WIN = 8
HALF = 4
EPS = 1e-05
MASKED = -1000000000.0
SCALE = HD**-0.5
CW = 256
CHUNK = 80
TOP = 48
F32 = jnp.float32
BF16 = jnp.bfloat16
MESH = pl.DeviceIdType.MESH


def dot(a, b):
    return lax.dot_general(a, b, (((1,), (0,)), ((), ())), preferred_element_type=F32)


def dot_t(a, b):
    return lax.dot_general(a, b, (((1,), (1,)), ((), ())), preferred_element_type=F32)


def t_dot(a, b):
    return lax.dot_general(a, b, (((0,), (0,)), ((), ())), preferred_element_type=F32)


def iota(shape, dim):
    return lax.broadcasted_iota(jnp.int32, shape, dim)


def stats(values):
    center = jnp.sum(values, axis=-1, keepdims=True) * (1.0 / C)
    shifted = values - center
    spread = jnp.sum(shifted * shifted, axis=-1, keepdims=True) * (1.0 / C)
    inverse = lax.rsqrt(spread + EPS)
    return shifted * inverse, inverse


def norm_back(values, grad):
    hat, inverse = stats(values)
    mean_grad = jnp.sum(grad, axis=-1, keepdims=True) * (1.0 / C)
    mean_dot = jnp.sum(grad * hat, axis=-1, keepdims=True) * (1.0 / C)
    return inverse * (grad - mean_grad - hat * mean_dot)


def by_heads(values):
    lane_head = iota(values.shape, 1) // HD
    zero = jnp.zeros_like(values)
    return jnp.concatenate([jnp.where(lane_head == h, values, zero) for h in range(HEADS)], axis=0)


def gather_heads(stacked):
    lane_head = iota((64, C), 1) // HD
    total = jnp.zeros((64, C), F32)
    for h in range(HEADS):
        total = jnp.where(lane_head == h, stacked[h * 64 : h * 64 + 64], total)
    return total


def head_reduce(scores, reduce, fill):
    pieces = []
    for pair in range(3):
        part = scores[:, pair * 128 : pair * 128 + 128]
        first = iota(part.shape, 1) < 64
        low = reduce(jnp.where(first, part, fill), axis=-1, keepdims=True)
        high = reduce(jnp.where(first, fill, part), axis=-1, keepdims=True)
        pieces.append(jnp.where(first, low, high))
    return jnp.concatenate(pieces, axis=1)


def softmax_window(q, k_heads, z_q, z_heads, bias):
    scores = dot_t(q, k_heads) * SCALE + bias
    scores = jnp.where(dot_t(z_q, z_heads) > 0.5, scores, MASKED)
    exponent = jnp.exp(scores - head_reduce(scores, jnp.max, -jnp.inf))
    return exponent / head_reduce(exponent, jnp.sum, 0.0)


def tile_ids(ids):
    z = (iota(ids.shape, 1).astype(F32) == ids).astype(BF16)
    return z, jnp.concatenate([z] * HEADS, axis=0)


def gelu_parts(pre):
    cdf = 0.5 * (1.0 + lax.erf(pre * (1.0 / math.sqrt(2.0))))
    slope = cdf + pre * (jnp.exp(-0.5 * pre * pre) * (1.0 / math.sqrt(2.0 * math.pi)))
    return pre * cdf, slope


def split(values):
    high = values.astype(BF16)
    rest = values - high.astype(F32)
    middle = rest.astype(BF16)
    low = (rest - middle.astype(F32)).astype(BF16)
    return jnp.concatenate([high, middle, low], axis=0)


def joined(pieces):
    n = pieces.shape[0] // 3
    return pieces[0:n] + pieces[n : 2 * n] + pieces[2 * n :]


def offset_onehots(out_ref):
    lane = iota((1, 128), 1)
    row = iota((256, 128), 0)
    for ci in range(WIN):
        offset = jnp.where(lane < 120, (14 - lane // 8) * 15 + (ci - lane % 8 + 7), -1)
        out_ref[ci] = (row == offset).astype(BF16)


def spread_bias(R):
    R.tab[...] = jnp.zeros((16, 256), F32)
    for b in range(2):
        R.tab[b * 8 : b * 8 + 6, 0:225] = R.table[:, b, :]
    pieces = split(R.tab[...])
    per_column = [joined(dot(pieces, R.offsets[ci])) for ci in range(WIN)]
    first = iota((8, 128), 1) < 64
    for b in range(2):
        per_head = [
            jnp.concatenate([per_column[ci][b * 8 + h : b * 8 + h + 1] for ci in range(WIN)], axis=0)
            for h in range(HEADS)
        ]
        for ri in range(WIN):
            shift = (7 - ri) * 8
            for pair in range(3):
                low = pltpu.roll(per_head[2 * pair], (128 - shift) % 128, 1)
                high = pltpu.roll(per_head[2 * pair + 1], (64 - shift) % 128, 1)
                R.bias[b, ri * 8 : ri * 8 + 8, pair * 128 : pair * 128 + 128] = jnp.where(first, low, high)


def fold_bias(grad_ref, offsets):
    first = iota((8, 128), 1) < 64
    per_head = [jnp.zeros((8, 128), F32) for _ in range(HEADS)]
    for ri in range(WIN):
        shift = (7 - ri) * 8
        for pair in range(3):
            part = grad_ref[ri * 8 : ri * 8 + 8, pair * 128 : pair * 128 + 128]
            low = pltpu.roll(jnp.where(first, part, 0.0), shift % 128, 1)
            high = pltpu.roll(jnp.where(first, 0.0, part), (shift + 64) % 128, 1)
            per_head[2 * pair] = per_head[2 * pair] + low
            per_head[2 * pair + 1] = per_head[2 * pair + 1] + high
    total = jnp.zeros((8, 256), F32)
    for ci in range(WIN):
        rows = jnp.concatenate([per_head[h][ci : ci + 1] for h in range(HEADS)] + [jnp.zeros((2, 128), F32)], axis=0)
        total = total + joined(dot_t(split(rows), offsets[ci]))
    return total


def place():
    r = lax.axis_index("rows")
    c = lax.axis_index("cols")
    return r, c


class Net:
    def __init__(self):
        r, c = place()
        self.r, self.c = r, c
        self.x_lo, self.z = r // 8, r % 8
        self.y, self.x_hi, self.core = c // 4, (c // 2) % 2, c % 2
        self.x = self.x_hi * 2 + self.x_lo

    def near(self, dr, dc):
        return ((self.r + dr + 16) % 16, (self.c + dc + 32) % 32)

    def partner(self):
        return (self.r, self.c + 1 - 2 * self.core)

    def at_x(self, x):
        return ((x % 2) * 8 + self.z, self.y * 4 + (x // 2) * 2 + self.core)

    def at_y(self, y):
        return (self.r, y * 4 + self.x_hi * 2 + self.core)

    def at_z(self, z):
        return (self.x_lo * 8 + z, self.c)

    def everyone(self):
        peers = [self.near(dr, dc) for dr, dc in SIDES] + [self.partner()]
        peers += [self.at_x((self.x + d) % 4) for d in range(1, 4)]
        peers += [self.at_y((self.y + d) % 8) for d in range(1, 8)]
        peers += [self.at_z((self.z + d) % 8) for d in range(1, 8)]
        return peers


SIDES = ((-1, 0), (1, 0), (0, -1), (0, 1), (-1, -1), (-1, 1), (1, -1), (1, 1))
SIDE_ROWS = (128, 128, 64, 64, 16, 16, 16, 16)
BACK_ROWS = (128, 128, 32, 32, 16, 16, 16, 16)


def remote(src, dst, send, recv, device):
    return pltpu.make_async_remote_copy(
        src_ref=src, dst_ref=dst, send_sem=send, recv_sem=recv, device_id=device, device_id_type=MESH
    )


def body(*refs):
    R = types.SimpleNamespace(**jax.tree.unflatten(STRUCTURE, refs[COUNT:]))
    R.tokens, R.ids, R.upper, R.upper_ids, R.lower, R.lower_ids, R.cot = refs[:7]
    R.qkv_w, R.proj_w, R.inner_w, R.outer_w, R.table, R.token_grad, R.totals = refs[7:14]
    R.table_total = refs[14]
    N = Net()

    barrier = pltpu.get_barrier_semaphore()
    peers = N.everyone()
    for peer in peers:
        pl.semaphore_signal(barrier, inc=1, device_id=peer, device_id_type=MESH)

    setup(R)
    forward_one(R)
    pl.semaphore_wait(barrier, len(peers))
    exchange_forward(R, N)
    forward_two(R)
    attend_back_two(R)
    send_back(R, N)
    grads_of(R, N, 1)
    table_of(R, 1)
    receive_back(R, N)
    channel_back_one(R)
    start_x(R, N, 1)
    attend_back_one(R)
    start_y(R, N, 1)
    grads_of(R, N, 0)
    table_of(R, 0)
    start_table(R, N)
    finish_one(R)
    start_z(R, N, 1)
    start_x(R, N, 0)
    finish_z(R, N, 1)
    start_y(R, N, 0)
    start_z(R, N, 0)
    finish_z(R, N, 0)


def select_column(rows, order, ids):
    n = ids.shape[0]
    row_of, col_of = order
    pick = (iota((rows, n), 1) == row_of(iota((rows, n), 0))).astype(BF16)
    spread = dot(pick, ids.astype(F32).astype(BF16))
    keep = iota((rows, 32), 1) == col_of(iota((rows, 32), 0))
    column = jnp.sum(jnp.where(keep, spread, 0.0), axis=-1, keepdims=True)
    return jnp.broadcast_to(column, (rows, 128))


def setup(R):
    offset_onehots(R.offsets)
    spread_bias(R)
    for i, ref in enumerate((R.wq, R.wk, R.wv)):
        ref[0] = R.qkv_w[0][:, i * C : i * C + C]
    for r in range(8):
        row = R.tokens[r].astype(F32)
        for w in range(4):
            R.x1[w * 64 + r * 8 : w * 64 + r * 8 + 8, :] = row[w * 8 : w * 8 + 8]
    by_window = (lambda t: (t // 8) % 8, lambda t: (t // 64) * 8 + t % 8)
    by_row = (lambda t: t // 32, lambda t: t % 32)
    R.id1[...] = select_column(256, by_window, R.ids[...])
    R.rim_id[0] = select_column(128, by_row, R.upper_ids[...])
    R.rim_id[1] = select_column(128, by_row, R.lower_ids[...])


def setup_later(R):
    for i, ref in enumerate((R.wq, R.wk, R.wv)):
        ref[1] = R.qkv_w[1][:, i * C : i * C + C]
    R.cot_ext[...] = jnp.zeros_like(R.cot_ext)
    for r in range(8):
        R.cot_ext[r, 4:36, :] = R.cot[r].astype(F32)
    for a in range(2):
        for b in range(5):
            for i in range(4):
                t = (a * 5 + b) * 32 + i * 8
                R.g2[t : t + 8, :] = R.cot_ext[a * 4 + i, b * 8 : b * 8 + 8, :]
    lane = iota((1, 1024), 1)
    inside = lane % 128
    row = (lane // 128 % 2 * 8 + inside // 12) * 48 + lane // 256 * 12 + inside % 12
    row = jnp.where(inside < 96, row, -1)
    R.pick_hid[...] = (iota((HID, 1024), 0) == row).astype(BF16)
    lane = iota((1, 256), 1)
    inside = lane % 128
    row = jnp.where(inside < 96, lane // 128 * 96 + inside, -1)
    R.pick_ch[...] = (iota((C, 256), 0) == row).astype(BF16)
    out = iota((4 * CHUNK, 1), 0)
    q, k = out // CHUNK, out % CHUNK
    hid = (k - 48) // 6
    col = jnp.where(
        k < 18,
        18 * q + k,
        jnp.where(
            k < 24,
            72 + 6 * q + k - 18,
            jnp.where(k < 48, 96 + 24 * q + k - 24, 192 + 24 * hid + 6 * q + (k - 48 - 6 * hid)),
        ),
    )
    col = jnp.where(k < 72, col, -1)
    R.cut[...] = (iota((4 * CHUNK, 288), 1) == col).astype(BF16)


def forward_one(R):
    @pl.loop(0, 2)
    def _(i):
        at = pl.ds(pl.multiple_of(i * 128, 128), 128)
        normed = stats(R.x1[at, :])[0].astype(BF16)
        R.n1[at, :] = normed
        for ref, weight in ((R.q1, R.wq), (R.k1, R.wk), (R.v1, R.wv)):
            ref[at, :] = dot(normed, weight[0]).astype(BF16)

    @pl.loop(0, 2)
    def _(pair):
        done = []
        for w in (pair * 2, pair * 2 + 1):
            at = pl.ds(pl.multiple_of(w * 64, 64), 64)
            z, z_heads = tile_ids(R.id1[at, :])
            probs = softmax_window(R.q1[at, :], by_heads(R.k1[at, :]), z, z_heads, R.bias[0])
            mix = dot(probs.astype(BF16), by_heads(R.v1[at, :])).astype(BF16)
            done.append((at, probs, mix))
        for at, probs, mix in done:
            R.p1[at, :] = probs
            R.mix1[at, :] = mix

    @pl.loop(0, 2)
    def _(i):
        at = pl.ds(pl.multiple_of(i * 128, 128), 128)
        middle = (R.x1[at, :] + dot(R.mix1[at, :], R.proj_w[0])).astype(BF16).astype(F32)
        R.mid1[at, :] = middle
        normed = stats(middle)[0].astype(BF16)
        R.m1[at, :] = normed
        act, slope = gelu_parts(dot(normed, R.inner_w[0]))
        act = act.astype(BF16)
        R.act1[at, :] = act
        R.slope1[at, :] = slope
        R.first[at, :] = (middle + dot_t(act, R.outer_w[0])).astype(BF16).astype(F32)


def exchange_forward(R, N):
    ext = R.ext
    for w in range(4):
        for r in range(8):
            t = w * 64 + r * 8
            piece = jnp.concatenate([R.first[t : t + 8, :], R.id1[t : t + 8, 0:64]], axis=1)
            ext[4 + r, 4 + w * 8 : 12 + w * 8, :] = piece
    for i, rim in enumerate((R.upper, R.lower)):
        for r in range(4):
            row = rim[r].astype(F32)
            R.rim[i, r] = jnp.concatenate([row, R.rim_id[i, r * 32 : r * 32 + 32, 0:64]], axis=1)
    for side, top in ((0, 4), (1, 8)):
        for r in range(4):
            R.pack[r * 32 : r * 32 + 32, :] = ext[top + r, 4:36, :]
        R.fs[side][...] = R.pack[0:128, :].astype(BF16)
    for side, left in ((2, 4), (3, 32)):
        for r in range(4):
            R.pack[r * 4 : r * 4 + 4, :] = R.rim[0, r, left - 4 : left, :]
            R.pack[48 + r * 4 : 52 + r * 4, :] = R.rim[1, r, left - 4 : left, :]
        for r in range(8):
            R.pack[16 + r * 4 : 20 + r * 4, :] = ext[4 + r, left : left + 4, :]
        R.fs[side][...] = R.pack[0:64, :].astype(BF16)
    for side, top, left in ((4, 4, 4), (5, 4, 32), (6, 8, 4), (7, 8, 32)):
        for r in range(4):
            R.pack[r * 4 : r * 4 + 4, :] = ext[top + r, left : left + 4, :]
        R.fs[side][...] = R.pack[0:16, :].astype(BF16)
    copies = []
    for side, (dr, dc) in enumerate(SIDES):
        copies.append(
            remote(
                R.fs[side], R.fr[side], R.fsend.at[side], R.frecv.at[side], N.near(dr, dc)
            )
        )
        copies[-1].start()
    setup_later(R)
    for copy in copies:
        copy.wait()
    at_top = N.r == 0
    at_bottom = N.r == 15
    R.pack[...] = R.fr[1][...].astype(F32)
    for r in range(4):
        ext[r, 4:36, :] = jnp.where(at_top, R.rim[0, r], R.pack[r * 32 : r * 32 + 32, :])
    R.pack[...] = R.fr[0][...].astype(F32)
    for r in range(4):
        ext[12 + r, 4:36, :] = jnp.where(at_bottom, R.rim[1, r], R.pack[r * 32 : r * 32 + 32, :])
    for strip, above, below, left in ((3, 7, 5, 0), (2, 6, 4, 36)):
        R.pack[0:64, :] = R.fr[strip][...].astype(F32)
        R.pack[64:80, :] = R.fr[above][...].astype(F32)
        R.pack[80:96, :] = R.fr[below][...].astype(F32)
        for r in range(4):
            own = R.pack[r * 4 : r * 4 + 4, :]
            ext[r, left : left + 4, :] = jnp.where(at_top, own, R.pack[64 + r * 4 : 68 + r * 4, :])
            own = R.pack[48 + r * 4 : 52 + r * 4, :]
            ext[12 + r, left : left + 4, :] = jnp.where(at_bottom, own, R.pack[80 + r * 4 : 84 + r * 4, :])
        for r in range(8):
            ext[4 + r, left : left + 4, :] = R.pack[16 + r * 4 : 20 + r * 4, :]


def query_start(n):
    return n * 64 + (1 - n // 5) * 32


def forward_two(R):
    ext = R.ext
    for a in range(2):
        for b in range(5):
            for i in range(8):
                t = ((a * 5 + b) * 8 + i) * 8
                piece = ext[a * 8 + i, b * 8 : b * 8 + 8, :]
                R.x2[t : t + 8, :] = piece[:, 0:C]
                R.id2[t : t + 8, :] = jnp.broadcast_to(piece[:, C : C + 1], (8, 128))
    @pl.loop(0, 5)
    def _(i):
        at = pl.ds(pl.multiple_of(i * 128, 128), 128)
        normed = stats(R.x2[at, :])[0].astype(BF16)
        R.n2[at, :] = normed
        for ref, weight in ((R.k2, R.wk), (R.v2, R.wv)):
            ref[at, :] = dot(normed, weight[1]).astype(BF16)

    for n in range(10):
        start = query_start(n)
        R.nq2[n * 32 : n * 32 + 32, :] = R.n2[start : start + 32, :]
        R.xq2[n * 32 : n * 32 + 32, :] = R.x2[start : start + 32, :]
    R.q2[...] = dot(R.nq2[...], R.wq[1]).astype(BF16)

    @pl.loop(0, 5)
    def _(b):
        done = []
        for n, first in ((b, 32), (b + 5, 0)):
            keys = pl.ds(pl.multiple_of(n * 64, 64), 64)
            queries = pl.ds(pl.multiple_of(n * 32, 32), 32)
            within = pl.ds(pl.multiple_of(n * 64 + first, 32), 32)
            z_heads = tile_ids(R.id2[keys, :])[1]
            z = tile_ids(R.id2[within, :])[0]
            bias = R.bias[1, first : first + 32, :]
            probs = softmax_window(R.q2[queries, :], by_heads(R.k2[keys, :]), z, z_heads, bias)
            mix = dot(probs.astype(BF16), by_heads(R.v2[keys, :])).astype(BF16)
            done.append((queries, probs, mix))
        for queries, probs, mix in done:
            R.p2[queries, :] = probs
            R.mix2[queries, :] = mix

    @pl.loop(0, 2)
    def _(i):
        at = pl.ds(pl.multiple_of(i * 160, 32), 160)
        middle = (R.xq2[at, :] + dot(R.mix2[at, :], R.proj_w[1])).astype(BF16).astype(F32)
        normed = stats(middle)[0].astype(BF16)
        R.m2[at, :] = normed
        act, slope = gelu_parts(dot(normed, R.inner_w[1]))
        R.act2[at, :] = act.astype(BF16)
        grad_out = R.g2[at, :]
        grad_pre = (slope * dot(grad_out.astype(BF16), R.outer_w[1])).astype(BF16)
        R.pre2[at, :] = grad_pre
        grad_mid = (grad_out + norm_back(middle, dot_t(grad_pre, R.inner_w[1]))).astype(BF16)
        R.gm2[at, :] = grad_mid
        R.e2[at, :] = dot_t(grad_mid, R.proj_w[1]).astype(BF16)


def window_back(probs, e, q, k_heads, v_heads):
    grad_probs = dot_t(e, v_heads)
    grad_scores = probs * (grad_probs - head_reduce(grad_probs * probs, jnp.sum, 0.0))
    low = grad_scores.astype(BF16)
    grad_q = (dot(low, k_heads) * SCALE).astype(BF16)
    grad_k = (gather_heads(t_dot(low, q)) * SCALE).astype(BF16)
    grad_v = gather_heads(t_dot(probs.astype(BF16), e)).astype(BF16)
    return grad_scores, grad_q, grad_k, grad_v


def attend_back_two(R):
    R.gb[1] = jnp.zeros((64, 384), F32)

    @pl.loop(0, 5)
    def _(b):
        done = []
        for n in (b, b + 5):
            keys = pl.ds(pl.multiple_of(n * 64, 64), 64)
            queries = pl.ds(pl.multiple_of(n * 32, 32), 32)
            back = window_back(
                R.p2[queries, :],
                R.e2[queries, :],
                R.q2[queries, :],
                by_heads(R.k2[keys, :]),
                by_heads(R.v2[keys, :]),
            )
            done.append((keys, queries, back))
        for half, (keys, queries, back) in zip((32, 0), done):
            R.gb[1, half : half + 32, :] = R.gb[1, half : half + 32, :] + back[0]
            R.dq2[queries, :] = back[1]
            R.dk2[keys, :] = back[2]
            R.dv2[keys, :] = back[3]

    R.dnq2[...] = dot_t(R.dq2[...], R.wq[1])

    @pl.loop(0, 5)
    def _(i):
        at = pl.ds(pl.multiple_of(i * 128, 128), 128)
        R.dn2[at, :] = dot_t(R.dk2[at, :], R.wk[1]) + dot_t(R.dv2[at, :], R.wv[1])

    @pl.loop(0, 10)
    def _(n):
        queries = pl.ds(pl.multiple_of(n * 32, 32), 32)
        within = pl.ds(pl.multiple_of(query_start(n), 32), 32)
        R.dn2[within, :] = R.dn2[within, :] + R.dnq2[queries, :]

    @pl.loop(0, 5)
    def _(i):
        at = pl.ds(pl.multiple_of(i * 128, 128), 128)
        R.dn2[at, :] = norm_back(R.x2[at, :], R.dn2[at, :])

    @pl.loop(0, 10)
    def _(n):
        queries = pl.ds(pl.multiple_of(n * 32, 32), 32)
        within = pl.ds(pl.multiple_of(query_start(n), 32), 32)
        R.dn2[within, :] = R.dn2[within, :] + R.gm2[queries, :].astype(F32)


def back_copy(R, N, side):
    dr, dc = SIDES[side]
    return remote(R.bs[side], R.br[side], R.bsend.at[side], R.brecv.at[side], N.near(dr, dc))


def send_back(R, N):
    ext = R.dext
    for a in range(2):
        for b in range(5):
            for i in range(8):
                t = ((a * 5 + b) * 8 + i) * 8
                ext[a * 8 + i, b * 8 : b * 8 + 8, :] = R.dn2[t : t + 8, :]
    pack = R.pack
    for side, top in ((0, 0), (1, 12)):
        for r in range(4):
            pack[r * 32 : r * 32 + 32, 0:C] = ext[top + r, 4:36, :]
        R.bs[side][...] = pack[0:128, 0:C].astype(BF16)
    for side, left in ((2, 0), (3, 36)):
        for r in range(8):
            pack[r * 4 : r * 4 + 4, 0:C] = ext[4 + r, left : left + 4, :]
        R.bs[side][...] = pack[0:32, 0:C].astype(BF16)
    for side, top, left in ((4, 0, 0), (5, 0, 36), (6, 12, 0), (7, 12, 36)):
        for r in range(4):
            pack[r * 4 : r * 4 + 4, 0:C] = ext[top + r, left : left + 4, :]
        R.bs[side][...] = pack[0:16, 0:C].astype(BF16)
    for side in range(8):
        back_copy(R, N, side).start()


def receive_back(R, N):
    for side in range(8):
        back_copy(R, N, side).wait()
    ext, pack = R.dext, R.pack
    above = jnp.where(N.r == 0, 0.0, 1.0).astype(F32)
    below = jnp.where(N.r == 15, 0.0, 1.0).astype(F32)
    pack[...] = jnp.zeros_like(pack)
    for side, top, left, rows, cols, keep in (
        (1, 4, 4, 4, 32, above),
        (0, 8, 4, 4, 32, below),
        (3, 4, 4, 8, 4, None),
        (2, 4, 32, 8, 4, None),
        (7, 4, 4, 4, 4, above),
        (6, 4, 32, 4, 4, above),
        (5, 8, 4, 4, 4, below),
        (4, 8, 32, 4, 4, below),
    ):
        received = R.br[side][...].astype(F32)
        if keep is not None:
            received = jnp.where(keep > 0.5, received, 0.0)
        pack[0 : BACK_ROWS[side], 0:C] = received
        for r in range(rows):
            ext[top + r, left : left + cols, :] = (
                ext[top + r, left : left + cols, :] + pack[r * cols : r * cols + cols, 0:C]
            )
    for w in range(4):
        for r in range(8):
            t = w * 64 + r * 8
            R.g1[t : t + 8, :] = ext[4 + r, 4 + w * 8 : 12 + w * 8, :]


def channel_back_one(R):
    @pl.loop(0, 2)
    def _(i):
        at = pl.ds(pl.multiple_of(i * 128, 128), 128)
        grad_out = R.g1[at, :].astype(BF16)
        R.gf1[at, :] = grad_out
        grad_pre = (R.slope1[at, :] * dot(grad_out, R.outer_w[0])).astype(BF16)
        R.pre1[at, :] = grad_pre
        back = norm_back(R.mid1[at, :], dot_t(grad_pre, R.inner_w[0]))
        grad_mid = (grad_out.astype(F32) + back).astype(BF16)
        R.gm1[at, :] = grad_mid
        R.e1[at, :] = dot_t(grad_mid, R.proj_w[0]).astype(BF16)


def attend_back_one(R):
    R.gb[0] = jnp.zeros((64, 384), F32)

    @pl.loop(0, 2)
    def _(pair):
        done = []
        for w in (pair * 2, pair * 2 + 1):
            at = pl.ds(pl.multiple_of(w * 64, 64), 64)
            back = window_back(
                R.p1[at, :], R.e1[at, :], R.q1[at, :], by_heads(R.k1[at, :]), by_heads(R.v1[at, :])
            )
            done.append((at, back))
        for at, back in done:
            R.gb[0] = R.gb[0] + back[0]
            R.dq1[at, :] = back[1]
            R.dk1[at, :] = back[2]
            R.dv1[at, :] = back[3]


def finish_one(R):
    @pl.loop(0, 2)
    def _(i):
        at = pl.ds(pl.multiple_of(i * 128, 128), 128)
        grad = dot_t(R.dq1[at, :], R.wq[0])
        grad = grad + dot_t(R.dk1[at, :], R.wk[0]) + dot_t(R.dv1[at, :], R.wv[0])
        R.x1[at, :] = R.gm1[at, :].astype(F32) + norm_back(R.x1[at, :], grad)

    for r in range(8):
        row = [R.x1[w * 64 + r * 8 : w * 64 + r * 8 + 8, :] for w in range(4)]
        R.token_grad[r] = jnp.concatenate(row, axis=0).astype(BF16)


def grads_of(R, N, b):
    pick = R.pick_ch[...]
    normed = dot((R.n1, R.n2)[b][...], pick).astype(BF16)
    query_normed = dot(R.nq2[...], pick).astype(BF16) if b else normed
    R.t_qkv[0:C, :] = t_dot((R.dq1, R.dq2)[b][...], query_normed)
    R.t_qkv[C : 2 * C, :] = t_dot((R.dk1, R.dk2)[b][...], normed)
    R.t_qkv[2 * C : 3 * C, :] = t_dot((R.dv1, R.dv2)[b][...], normed)
    R.t_proj[...] = t_dot((R.gm1, R.gm2)[b][...], dot((R.mix1, R.mix2)[b][...], pick).astype(BF16))
    R.t_inner[...] = t_dot((R.pre1, R.pre2)[b][...], dot((R.m1, R.m2)[b][...], pick).astype(BF16))
    grad_out = R.g2[...].astype(BF16) if b else R.gf1[...]
    for s in range(4):
        act = dot((R.act1, R.act2)[b][...], R.pick_hid[:, s * 256 : s * 256 + 256]).astype(BF16)
        R.t_outer[s] = t_dot(grad_out, act)

    @pl.loop(0, 8)
    def _(y):
        def part(ref, width):
            return ref[pl.ds(pl.multiple_of(y * width, 8), width), :]

        stacked = [part(R.t_qkv, 72), part(R.t_proj, 24), part(R.t_inner, 96)]
        stacked += [part(R.t_outer.at[s], 24) for s in range(4)]
        chunks = dot(R.cut[...], jnp.concatenate(stacked, axis=0).astype(BF16)).astype(BF16)
        for q in range(4):
            for x_lo in range(2):
                R.ga[b, q % 2, q // 2 * 2 + x_lo, y] = chunks[
                    q * CHUNK : q * CHUNK + CHUNK, x_lo * 128 : x_lo * 128 + 128
                ]
        core_copy(R, N, b, y).start()


def table_of(R, b):
    R.tab[b * 8 : b * 8 + 8, :] = fold_bias(R.gb.at[b], R.offsets)


def core_copy(R, N, b, y):
    at = b * 8 + y
    return remote(
        R.ga.at[b, 1 - N.core, :, y], R.ra.at[b, :, y], R.asend.at[at], R.arecv.at[at], N.partner()
    )


def start_table(R, N):
    R.ta[...] = R.tab[...].astype(BF16)
    table_copy(R, N).start()


def table_copy(R, N):
    return remote(R.ta, R.rta, R.tsend.at[0], R.trecv.at[0], N.partner())


def spread_copies(R, send, recv, src, dst, base, me, n, device):
    def sending(other, d):
        return remote(src(other), dst(me), send.at[base + d], recv.at[base + me], device(other))

    def arriving(other, d):
        return remote(src(other), dst(other), send.at[base + d], recv.at[base + other], device(other))

    return [(functools.partial(sending, (me + d) % n, d), functools.partial(arriving, (me + d) % n, d)) for d in range(1, n)]


def x_copies(R, N, b):
    def source(other):
        return R.hb.at[b, other, :, 0:TOP, :]

    return spread_copies(R, R.xsend, R.xrecv, source, lambda s: R.rb.at[b, s], b * 4, N.x, 4, N.at_x)


def y_copies(R, N, b):
    return spread_copies(
        R, R.ysend, R.yrecv, lambda o: R.hc.at[b, o], lambda s: R.rc.at[b, s], b * 8, N.y, 8, N.at_y
    )


def y_first_copies(R, N, b):
    def source(other):
        return R.hb.at[b, :, other, TOP:CHUNK, :]

    return spread_copies(R, R.vsend, R.vrecv, source, lambda s: R.rv.at[b, s], b * 8, N.y, 8, N.at_y)


def x_second_copies(R, N, b):
    return spread_copies(
        R, R.wsend, R.wrecv, lambda o: R.hw.at[b, o], lambda s: R.rw.at[b, s], b * 4, N.x, 4, N.at_x
    )


def z_copies(R, N, b):
    return spread_copies(
        R, R.zsend, R.zrecv, lambda o: R.hd.at[b, o], lambda s: R.rd.at[b, s], b * 8, N.z, 8, N.at_z
    )


def table_copies(R, N, stage):
    me, n, device = ((N.x, 4, N.at_x), (N.y, 8, N.at_y), (N.z, 8, N.at_z))[stage]
    base = stage * 8
    src, dst = R.table_out[stage], R.table_in[stage]
    return spread_copies(
        R, R.tbsend, R.tbrecv, lambda o: src, lambda s: dst.at[s], base, me, n, device
    )


def go(copies):
    for sending, _ in copies:
        sending().start()


def settle(copies):
    for sending, arriving in copies:
        sending().wait_send()
        arriving().wait_recv()


def table_sum(R, N, stage):
    settle(table_copies(R, N, stage))
    n = 8 if stage else 4
    received = R.table_in[stage]
    total = received[0].astype(F32)
    for s in range(1, n):
        total = total + received[s].astype(F32)
    return total


def table_send(R, N, stage, total):
    me = (N.x, N.y, N.z)[stage]
    low = total.astype(BF16)
    R.table_out[stage][...] = low
    R.table_in[stage][me] = low
    go(table_copies(R, N, stage))


def start_x(R, N, b):
    for y in range(8):
        core_copy(R, N, b, y).wait()

    over_x = x_copies(R, N, b)
    for d in (1, 3, 2, 0):
        x = (N.x + d) % 4
        for y in range(8):
            total = R.ga[b, N.core, x, y].astype(F32) + R.ra[b, x, y].astype(F32)
            R.hb[b, x, y] = total.astype(BF16)
        if d:
            go(over_x[d - 1 : d])
    go(y_first_copies(R, N, b))
    if b == 0:
        table_copy(R, N).wait()
        table_send(R, N, 0, R.ta[...].astype(F32) + R.rta[...].astype(F32))


def start_y(R, N, b):
    settle(x_copies(R, N, b))

    @pl.loop(0, 8)
    def _(y):
        total = R.hb[b, N.x, y, 0:TOP, :].astype(F32)
        for d in range(1, 4):
            total = total + R.rb[b, (N.x + d) % 4, y].astype(F32)
        R.hc[b, y] = total.astype(BF16)

    go(y_copies(R, N, b))
    settle(y_first_copies(R, N, b))
    for x in range(4):
        total = R.hb[b, x, N.y, TOP:CHUNK, :].astype(F32)
        for d in range(1, 8):
            total = total + R.rv[b, (N.y + d) % 8, x].astype(F32)
        R.hw[b, x] = total.astype(BF16)
    go(x_second_copies(R, N, b))
    if b == 0:
        table_send(R, N, 1, table_sum(R, N, 0))


def start_z(R, N, b):
    settle(y_copies(R, N, b))
    total = R.hc[b, N.y].astype(F32)
    for d in range(1, 8):
        total = total + R.rc[b, (N.y + d) % 8].astype(F32)
    settle(x_second_copies(R, N, b))
    rest = R.hw[b, N.x].astype(F32)
    for d in range(1, 4):
        rest = rest + R.rw[b, (N.x + d) % 4].astype(F32)
    R.turn[...] = jnp.concatenate([total, rest, jnp.zeros((128 - CHUNK, 128), F32)], axis=0).T
    for z in range(8):
        R.hd[b, z] = R.turn[z * 12 : z * 12 + 16, :].astype(BF16)
    go(z_copies(R, N, b))
    if b == 0:
        table_send(R, N, 2, table_sum(R, N, 1))


def finish_z(R, N, b):
    settle(z_copies(R, N, b))
    total = R.hd[b, N.z].astype(F32)
    for d in range(1, 8):
        total = total + R.rd[b, (N.z + d) % 8].astype(F32)
    R.totals[b] = total
    if b == 0:
        R.table_total[...] = table_sum(R, N, 2)


def hand_on(summed, totals, table, tokens, qkv, proj, inner, outer, table_grad):
    tokens[...] = summed[...]
    for b in range(2):
        total = totals[b] * (1.0 / 512.0)
        qkv[:, b, :] = total[0:12, 0:18]
        inner[:, b, :] = total[0:12, 24:48]
        turned = jnp.concatenate([total, jnp.zeros((112, 128), F32)], axis=0).T
        proj[:, b, :] = turned[18:24, 0:12]
        parts = [turned[48 + 6 * s : 54 + 6 * s, 0:12] for s in range(4)]
        outer[:, b, :] = jnp.concatenate(parts, axis=1)
        table_grad[:, b, :] = table[b * 8 : b * 8 + 6, 0:225] * (1.0 / 512.0)


def scratch():
    def f(*shape):
        return pltpu.VMEM(shape, F32)

    def h(*shape):
        return pltpu.VMEM(shape, BF16)

    def semaphores(count):
        return pltpu.SemaphoreType.DMA((count,))

    out = dict(wq=h(2, C, C), wk=h(2, C, C), wv=h(2, C, C), bias=f(2, 64, 384))
    out.update(x1=f(256, C), id1=f(256, 128), rim_id=f(2, 128, 128), rim=f(2, 4, 32, CW))
    out.update(pick_hid=h(HID, 1024), pick_ch=h(C, 256), cut=h(4 * CHUNK, 288))
    out.update(n1=h(256, C), q1=h(256, C), k1=h(256, C), v1=h(256, C), mix1=h(256, C), m1=h(256, C))
    out.update(gf1=h(256, C), gm1=h(256, C), e1=h(256, C), dq1=h(256, C), dk1=h(256, C), dv1=h(256, C))
    out.update(p1=f(256, 384), mid1=f(256, C), first=f(256, C), g1=f(256, C))
    out.update(act1=h(256, HID), slope1=f(256, HID), pre1=h(256, HID))
    out.update(ext=f(16, 40, CW), dext=f(16, 40, C), cot_ext=f(8, 40, C), pack=f(128, CW))
    out.update(x2=f(640, C), id2=f(640, 128), dn2=f(640, C))
    out.update(n2=h(640, C), k2=h(640, C), v2=h(640, C), dk2=h(640, C), dv2=h(640, C))
    out.update(nq2=h(320, C), q2=h(320, C), mix2=h(320, C), m2=h(320, C), gm2=h(320, C), e2=h(320, C), dq2=h(320, C))
    out.update(xq2=f(320, C), g2=f(320, C), dnq2=f(320, C), p2=f(320, 384))
    out.update(act2=h(320, HID), pre2=h(320, HID), gb=f(2, 64, 384))
    out.update(t_qkv=f(576, 256), t_proj=f(C, 256), t_inner=f(HID, 256), t_outer=f(4, C, 256))
    out.update(offsets=h(WIN, 256, 128), tab=f(16, 256), turn=f(128, 128))
    out.update(fs=[h(n, CW) for n in SIDE_ROWS], fr=[h(n, CW) for n in SIDE_ROWS])
    out.update(bs=[h(n, C) for n in BACK_ROWS], br=[h(n, C) for n in BACK_ROWS])
    out.update(ga=h(2, 2, 4, 8, CHUNK, 128), ra=h(2, 4, 8, CHUNK, 128))
    out.update(hb=h(2, 4, 8, CHUNK, 128), rb=h(2, 4, 8, TOP, 128))
    out.update(rv=h(2, 8, 4, CHUNK - TOP, 128), hw=h(2, 4, CHUNK - TOP, 128), rw=h(2, 4, CHUNK - TOP, 128))
    out.update(hc=h(2, 8, TOP, 128), rc=h(2, 8, TOP, 128), hd=h(2, 8, 16, 128), rd=h(2, 8, 16, 128))
    out.update(ta=h(16, 256), rta=h(16, 256), table_out=[h(16, 256)] * 3)
    out.update(table_in=[h(4, 16, 256), h(8, 16, 256), h(8, 16, 256)])
    out.update(fsend=semaphores(8), frecv=semaphores(8), bsend=semaphores(8), brecv=semaphores(8))
    out.update(asend=semaphores(16), arecv=semaphores(16), tsend=semaphores(1), trecv=semaphores(1))
    out.update(xsend=semaphores(8), xrecv=semaphores(8), ysend=semaphores(16), yrecv=semaphores(16))
    out.update(zsend=semaphores(16), zrecv=semaphores(16), tbsend=semaphores(24), tbrecv=semaphores(24))
    out.update(vsend=semaphores(16), vrecv=semaphores(16), wsend=semaphores(8), wrecv=semaphores(8))
    return out


SHAPES, STRUCTURE = jax.tree.flatten(scratch(), is_leaf=lambda x: not isinstance(x, (dict, list)))
COUNT = 15


def local(
    tokens,
    region_ids,
    upper_rim,
    upper_ids,
    lower_rim,
    lower_ids,
    cotangent,
    qkv_weight,
    proj_weight,
    inner_weight,
    outer_weight,
    bias_table,
):
    out = pl.pallas_call(
        body,
        out_shape=(
            jax.ShapeDtypeStruct((8, 32, C), BF16),
            jax.ShapeDtypeStruct((2, 16, 128), F32),
            jax.ShapeDtypeStruct((16, 256), F32),
        ),
        in_specs=[pl.BlockSpec(memory_space=pltpu.VMEM)] * 12,
        out_specs=[pl.BlockSpec(memory_space=pltpu.VMEM)] * 3,
        scratch_shapes=SHAPES,
        compiler_params=pltpu.CompilerParams(
            collective_id=0, has_side_effects=True, vmem_limit_bytes=60 * 1024 * 1024
        ),
        name="blocks",
    )(
        tokens,
        region_ids,
        upper_rim,
        upper_ids,
        lower_rim,
        lower_ids,
        cotangent,
        qkv_weight,
        proj_weight,
        inner_weight,
        outer_weight.transpose(0, 2, 1),
        bias_table.transpose(2, 0, 1),
    )
    out = pl.pallas_call(
        hand_on,
        out_shape=(
            jax.ShapeDtypeStruct((8, 32, C), BF16),
            jax.ShapeDtypeStruct((12, 2, 18), F32),
            jax.ShapeDtypeStruct((6, 2, 12), F32),
            jax.ShapeDtypeStruct((12, 2, 24), F32),
            jax.ShapeDtypeStruct((6, 2, 48), F32),
            jax.ShapeDtypeStruct((6, 2, 225), F32),
        ),
        in_specs=[pl.BlockSpec(memory_space=pltpu.VMEM)] * 3,
        out_specs=[pl.BlockSpec(memory_space=pltpu.VMEM)] * 6,
        name="hand_on",
    )(*out)
    orders = ((1, 0, 2), (1, 2, 0), (1, 0, 2), (1, 2, 0), (1, 2, 0))
    return (out[0], *(part.transpose(order) for part, order in zip(out[1:], orders)))


def solution(mesh):
    return jax.shard_map(
        local,
        mesh=mesh,
        in_specs=(
            P("rows", "cols", None),
            P("rows", "cols"),
            P(None, "cols", None),
            P(None, "cols"),
            P(None, "cols", None),
            P(None, "cols"),
            P("rows", "cols", None),
            P(),
            P(),
            P(),
            P(),
            P(),
        ),
        out_specs=(
            P("rows", "cols", None),
            P(None, "rows", "cols"),
            P(None, "rows", "cols"),
            P(None, "rows", "cols"),
            P(None, "rows", "cols"),
            P(),
        ),
        check_vma=False,
    )
```
